128 devices in a mesh: layer: 8 (over x, z_lo), tok: 16 (over y, z_hi, core).
Axes of the slice: x: 4, y: 4, z: 4 (z_hi: 2, z_lo: 2; z = z_hi * 2 + z_lo), core: 2. Of those that a mesh axis runs over, the one named last changes fastest.
Arguments:
- layer_inputs: bfloat16 [8, 512, 2048], P('layer', 'tok'), may hold values from -6 to 6
- layer_targets: bfloat16 [8, 512, 2048], P('layer', 'tok'), may hold values from -12 to 12
- row_order: int32 [512], replicated, may hold values from 0 to 511, each once
- encoder_weight: bfloat16 [8, 2048, 4096], P('layer', None, 'tok'), may hold values from -0.125 to 0.125
- encoder_bias: float32 [8, 4096], P('layer', 'tok'), may hold values from -3 to 3
- decoder_weight: bfloat16 [8, 8, 4096, 2048], P('layer', None, 'tok'), may hold values from -1 to 1
- decoder_bias: float32 [8, 2048], P('layer'), may hold values from -0.6 to 0.6
Outputs:
- encoder_grad: bfloat16 [8, 2048, 4096], P('layer', None, 'tok')
- feature_grad: float32 [8, 4096], P('layer', 'tok')
- decoder_grad: bfloat16 [8, 8, 4096, 2048], P('layer', None, 'tok')
- output_grad: float32 [8, 2048], P('layer')
The draws below stay inside these ranges and needn't reach their ends.
Inputs may be any that keep to these rules, and one draw needn't show every extreme that they name: Row i of layer_targets belongs to the token in row row_order[i] of layer_inputs, in every layer; each row index appears once.
All inputs are finite; a program needn't handle non-finite values.
Results may differ from the reference program's by a relative error of at most 0.015.
Values may be sent and summed in bfloat16 or wider, within the bound.
A program may use at most 128 MiB of HBM per device.

```python
import math
import jax
import jax.numpy as jnp
from jax import lax

D = 2048
FC = 4096
L = 8
TOKENS = 512


def draw_decoder_weight(key, part):
    subkeys = jax.random.split(key, 3)
    shape = (L, L, FC, D)
    base_noise = jnp.clip(jax.random.normal(subkeys[0], shape, jnp.float32), -4.0, 4.0)
    growth = 3.0
    row_scale = jnp.exp(jax.random.uniform(subkeys[1], (L, L, FC, 1), jnp.float32, -1.1513, 1.1513))
    col_scale = jnp.exp(jax.random.uniform(subkeys[2], (L, 1, 1, D), jnp.float32, -1.1513, 1.1513))
    layer_index = jnp.arange(L).astype(jnp.float32)
    layer_scale = growth ** (layer_index / max(L - 1, 1)) / jnp.sqrt(FC * (layer_index + 1.0))
    values = base_noise * row_scale * col_scale * layer_scale.reshape(L, 1, 1, 1)
    return jnp.clip(values, -1.0, 1.0).astype(jnp.bfloat16)


def level_of(stream_key, extent, cuts, low, top_value):
    factor_of = 1.0
    for position, blocks in cuts:
        steps = jax.random.uniform(jax.random.fold_in(jax.random.fold_in(stream_key, 6), position), (blocks,), jnp.float32, low / len(cuts), top_value / len(cuts))
        factor_of = factor_of * jnp.repeat(jnp.exp(steps), extent[position] // blocks).reshape((-1,) + (1,) * (len(extent) - 1 - position))
    return factor_of


def scatter_about(stream_key, dims, scale, bound, pieces=(), held_as=jnp.bfloat16):
    result = jax.random.normal(stream_key, dims, jnp.float32) * scale
    if len(pieces) > 0:
        result = level_of(stream_key, dims, pieces, -0.22, 0.18) * result
    return jnp.clip(result, min=-bound, max=bound).astype(held_as)


def setup_inputs(seed: int = 0) -> dict:
    key_list = jax.random.split(jax.random.key(seed), 8)
    return {
        "layer_inputs": scatter_about(key_list[0], (L, TOKENS, D), 1.0, 6.0, ((0, 8), (1, 16))),
        "layer_targets": scatter_about(key_list[1], (L, TOKENS, D), 2.0, 12.0, ((0, 8), (1, 16))),
        "row_order": jax.random.permutation(key_list[2], TOKENS).astype(jnp.int32),
        "encoder_weight": scatter_about(key_list[3], (L, D, FC), D ** -0.5, 0.125, ((0, 8), (2, 16))),
        "encoder_bias": scatter_about(key_list[4], (L, FC), 0.5, 3.0, ((0, 8), (1, 16)), jnp.float32),
        "decoder_weight": draw_decoder_weight(jax.random.fold_in(key_list[7], 71), 0),
        "decoder_bias": scatter_about(key_list[6], (L, D), 0.1, 0.6, ((0, 8),), jnp.float32),
    }


def reference(layer_inputs, layer_targets, row_order, encoder_weight, encoder_bias, decoder_weight, decoder_bias):
    layers = layer_inputs.shape[0]
    row_total = layer_inputs.shape[1]
    width = layer_inputs.shape[2]
    features = encoder_weight.shape[2]
    loss_scale = 1.0 / math.sqrt(row_total)
    contract_rows = (((0,), (0,)), ((), ()))
    contract_cols = (((1,), (1,)), ((), ()))
    ordered_list = []
    pre_list = []
    act_list = []
    norm_list = []
    for source in range(layers):
        ordered = jnp.take(layer_inputs[source], row_order.astype(jnp.int32), axis=0)
        pre_act = jnp.dot(ordered, encoder_weight[source], preferred_element_type=jnp.float32) + encoder_bias[source]
        ordered_list.append(ordered)
        pre_list.append(pre_act)
        act_list.append(jnp.maximum(pre_act, 0.0).astype(jnp.bfloat16))
        squares = jnp.zeros((features,), jnp.float32)
        for target in range(source, layers):
            squares = squares + lax.optimization_barrier(jnp.sum(jnp.square(decoder_weight[target, source].astype(jnp.float32)), axis=1))
        norm_list.append(jnp.sqrt(squares + 1e-06))
    resid_list = []
    output_rows = []
    for target in range(layers):
        decoded = jnp.zeros((row_total, width), jnp.float32)
        for source in range(target + 1):
            decoded = decoded + jnp.dot(act_list[source], decoder_weight[target, source], preferred_element_type=jnp.float32)
        resid_full = (decoded + decoder_bias[target] - layer_targets[target].astype(jnp.float32)) * loss_scale
        output_rows.append(lax.optimization_barrier(jnp.sum(resid_full, axis=0)))
        resid_list.append(resid_full.astype(jnp.bfloat16))
    encoder_rows = []
    feature_rows = []
    decoder_rows = []
    for source in range(layers):
        grad_acts = jnp.zeros((row_total, features), jnp.float32)
        for target in range(source, layers):
            grad_acts = grad_acts + lax.dot_general(resid_list[target], decoder_weight[target, source], contract_cols, preferred_element_type=jnp.float32)
        grad_pre = jnp.where(pre_list[source] > 0, grad_acts + norm_list[source] * loss_scale, 0.0)
        grad_low = grad_pre.astype(jnp.bfloat16)
        encoder_rows.append(lax.dot_general(ordered_list[source], grad_low, contract_rows, preferred_element_type=jnp.float32).astype(jnp.bfloat16))
        feature_rows.append(lax.optimization_barrier(jnp.sum(grad_pre, axis=0)))
    for target in range(layers):
        blocks = []
        for source in range(layers):
            if source <= target:
                act_sums = lax.optimization_barrier(jnp.sum(act_list[source].astype(jnp.float32), axis=0))
                factor = act_sums * loss_scale / norm_list[source]
                product = lax.dot_general(act_list[source], resid_list[target], contract_rows, preferred_element_type=jnp.float32)
                blocks.append((product + factor[:, None] * decoder_weight[target, source].astype(jnp.float32)).astype(jnp.bfloat16))
            else:
                blocks.append(jnp.zeros((features, width), jnp.bfloat16))
        decoder_rows.append(jnp.stack(blocks))
    return (jnp.stack(encoder_rows), jnp.stack(feature_rows), jnp.stack(decoder_rows), jnp.stack(output_rows))
```

```python
import math

import jax
import jax.numpy as jnp
from jax import lax
from jax.experimental import pallas as pl
from jax.experimental.pallas import tpu as pltpu
from jax.sharding import PartitionSpec as P

MESH = pl.DeviceIdType.MESH
F32, BF16 = jnp.float32, jnp.bfloat16
NT_DIMS = (((1,), (1,)), ((), ()))
TN_DIMS = (((0,), (0,)), ((), ()))

LAYERS = 8
TOKS = 16
ROWS = 512
D = 2048
FS = 256
CH = 2
PR = 16
CR = TOKS * PR
NT = 512
NSTEPS = D // NT
SCALE = 1.0 / math.sqrt(ROWS)


def main_kernel(
    x_hbm, t_hbm, order_ref, we_hbm, eb_ref, w_hbm, db_ref,
    xo_hbm, ao_hbm, ro_hbm, go_hbm, no_ref,
    xbuf, tbuf, rbuf, acts, pact, bact, pre, we, w,
    opart, sibs, sibr, ys, yr, zs, zr, dkeep,
    gb, gown, frecv, fzs, fzr, gtot, nrecv, gl,
    lsem, osem, ag_s, ag_r, b_s, b_r, cs_s, cs_r, cy_s, cy_r, cz_s, cz_r,
    f_s, f_r, fz_s, fz_r, n_s, n_r,
):
    m, t = lax.axis_index("layer"), lax.axis_index("tok")
    x, zl = m // 2, m % 2
    y, zh, c = t // 4, (t // 2) % 2, t % 2
    yp, ym, yo = (y + 1) % 4, (y + 3) % 4, (y + 2) % 4
    xp, xm = (x + 1) % 4, (x + 3) % 4

    def tk(yy, zz, cc):
        return 4 * yy + 2 * zz + cc

    def by_core(yy, zz, cc):
        return 8 * cc + 2 * yy + zz

    sib, zpt = (m, tk(y, zh, 1 - c)), (m, tk(y, 1 - zh, c))
    yup, ydn = (m, tk(yp, zh, c)), (m, tk(ym, zh, c))
    xup, xdn = (2 * xp + zl, t), (2 * xm + zl, t)
    mp = m + 1 - 2 * zl
    zpl = (mp, t)

    def remote(src, dst, s, r, dev):
        return pltpu.make_async_remote_copy(
            src_ref=src, dst_ref=dst, send_sem=s, recv_sem=r, device_id=dev, device_id_type=MESH
        )

    acts[...] = jnp.zeros_like(acts)

    local = []

    def fetch(src, dst, k):
        cp = pltpu.make_async_copy(src, dst, lsem.at[k])
        cp.start()
        local.append(cp)

    own_core = by_core(y, zh, c)
    for r in range(CH):
        fetch(x_hbm.at[0, pl.ds(r * PR, PR)], xbuf.at[r, own_core], r)
    fetch(we_hbm.at[0], we, 2)
    fetch(t_hbm.at[0], tbuf.at[t], 3)
    for l in range(LAYERS):
        fetch(w_hbm.at[0, l], w.at[pl.ds(l * FS, FS)], 4 + l)

    barrier = pltpu.get_barrier_semaphore()
    for dev in (sib, zpt, yup, ydn):
        pl.semaphore_signal(barrier, inc=1, device_id=dev, device_id_type=MESH)
    for k in range(1, LAYERS):
        pl.semaphore_signal(barrier, inc=1, device_id=((m + k) % LAYERS, t), device_id_type=MESH)
    pl.semaphore_wait(barrier, 4 + LAYERS - 1)

    sent = []

    class Gather:
        def __init__(self, inst, at, own_src, slot):
            self.inst, self.at, self.own_src, self.slot, self.k = inst, at, own_src, slot, 0

        def send(self, src, slot, dev):
            cp = remote(src, self.at(slot), ag_s.at[self.inst, self.k], ag_r.at[self.inst, slot], dev)
            cp.start()
            sent.append(cp)
            self.k += 1

        def wait(self, slot):
            remote(self.at(slot), self.at(slot), ag_s.at[self.inst, 0], ag_r.at[self.inst, slot], sib).wait_recv()

        def pass_on(self, slot, *devs):
            self.wait(slot)
            for dev in devs:
                self.send(self.at(slot), slot, dev)

        def start(self):
            own = self.slot(y, zh, c)
            for dev in (zpt, yup, ydn, sib):
                self.send(self.own_src, own, dev)

        def relay1(self):
            self.pass_on(self.slot(y, 1 - zh, c), yup, ydn, sib)

        def relay2(self):
            self.pass_on(self.slot(ym, zh, c), yup, sib)
            self.pass_on(self.slot(yp, 1 - zh, c), ydn, sib)
            self.pass_on(self.slot(yp, zh, c), sib)
            self.pass_on(self.slot(ym, 1 - zh, c), sib)

        def finish(self):
            self.pass_on(self.slot(yo, zh, c), sib)
            self.pass_on(self.slot(yo, 1 - zh, c), sib)
            for yy in range(4):
                for zz in range(2):
                    self.wait(self.slot(yy, zz, 1 - c))

    ax = [
        Gather(r, (lambda s, r=r: xbuf.at[r, s]), x_hbm.at[0, pl.ds(r * PR, PR)], by_core)
        for r in range(CH)
    ]
    at = Gather(2, (lambda s: tbuf.at[s]), t_hbm.at[0], tk)
    ar = [
        Gather(3 + r, (lambda s, r=r: rbuf.at[r, s]), rbuf.at[r, own_core], by_core)
        for r in range(CH)
    ]

    outs = []

    def put(src, dst, k):
        cp = pltpu.make_async_copy(src, dst, osem.at[k])
        cp.start()
        outs.append(cp)

    def encode(r):
        rows = xbuf[r].reshape(CR, D)
        value = jnp.dot(rows, we[...], preferred_element_type=F32) + eb_ref[...]
        pre[r] = value
        acts[r, :, pl.ds(pl.multiple_of(m * FS, FS), FS)] = jnp.maximum(value, 0.0).astype(BF16)

    def act_at(r, l):
        return acts.at[r, :, pl.ds(pl.multiple_of(l * FS, FS), FS)]

    def b_copy(r, k, src, dst, slot, dev):
        return remote(src, dst, b_s.at[r, k], b_r.at[r, slot], dev)

    def b_wait(r, l):
        b_copy(r, 0, act_at(r, l), act_at(r, l), l, sib).wait_recv()

    def b_own(r):
        return [
            (None, b_copy(r, 0, act_at(r, m), pact.at[r], 8, zpl)),
            (x < 3, b_copy(r, 1, act_at(r, m), act_at(r, m), m, xup)),
            (x == 0, b_copy(r, 2, act_at(r, m), act_at(r, m), m, xdn)),
            (m == 3, b_copy(r, 3, act_at(r, m), bact.at[r], 9, xdn)),
        ]

    def b_partner(r):
        return [
            (x < 3, b_copy(r, 4, pact.at[r], act_at(r, mp), mp, xup)),
            (x == 0, b_copy(r, 5, pact.at[r], act_at(r, mp), mp, xdn)),
            (m == 2, b_copy(r, 6, pact.at[r], bact.at[r], 9, xdn)),
        ]

    def b_relay(r):
        return [
            (x == 0, (9,), [b_copy(r, 7, bact.at[r], act_at(r, 3), 3, xdn)]),
            (x == 2, (2,), [b_copy(r, 7, act_at(r, 2), act_at(r, 2), 2, xup)]),
            (x == 3, (0, 1), [b_copy(r, 7 + l, act_at(r, l), act_at(r, l), l, xdn) for l in (0, 1)]),
        ]

    def when(cond, fn):
        if cond is None:
            fn()
        else:
            pl.when(cond)(fn)

    def b_start(r):
        for cond, cp in b_own(r):
            when(cond, cp.start)

    def b_step1(r):
        remote(pact.at[r], pact.at[r], b_s.at[r, 0], b_r.at[r, 8], sib).wait_recv()
        for cond, cp in b_partner(r):
            when(cond, cp.start)

        @pl.when(zl == 1)
        def _():
            acts[r, :, pl.ds(pl.multiple_of(mp * FS, FS), FS)] = pact[r]

    def b_step2(r):
        for cond, slots, copies in b_relay(r):

            def go(slots=slots, copies=copies):
                for slot, cp in zip(slots, copies):
                    if slot == 9:
                        remote(bact.at[r], bact.at[r], b_s.at[r, 0], b_r.at[r, 9], sib).wait_recv()
                    else:
                        b_wait(r, slot)
                    cp.start()

            when(cond, go)

    def b_finish(r):
        for cond, slots in ((x == 1, (0, 1)), (x == 2, (0, 1, 3)), (x == 3, (2, 3, 4, 5))):
            when(cond, lambda slots=slots: [b_wait(r, l) for l in slots] and None)

    def b_drain(r):
        for cond, cp in b_own(r) + b_partner(r):
            when(cond, cp.wait_send)
        for cond, _, copies in b_relay(r):
            when(cond, lambda copies=copies: [cp.wait_send() for cp in copies] and None)

    def norm_copy(k):
        return remote(nrecv.at[m], nrecv.at[m], n_s.at[k], n_r.at[m], ((m + k) % LAYERS, t))

    def norms():
        for k in range(4, 4 + LAYERS):
            local[k].wait()

        @pl.loop(0, LAYERS)
        def _(l):
            part = jnp.zeros((FS, 128), F32)
            for j in range(D // 128):
                v = w[pl.ds(pl.multiple_of(l * FS, FS), FS), j * 128 : (j + 1) * 128].astype(F32)
                part = part + v * v
            row = lax.dot_general(
                jnp.ones((8, 128), F32), part, NT_DIMS,
                preferred_element_type=F32, precision=lax.Precision.HIGHEST,
            )
            keep = jnp.where(l <= m, 1.0, 0.0).astype(F32)
            nrecv[m, pl.ds(l, 1), :] = row[0:1] * keep

        for k in range(1, LAYERS):
            norm_copy(k).start()

    def norms_finish():
        for k in range(1, LAYERS):
            s = (m + k) % LAYERS
            remote(nrecv.at[s], nrecv.at[s], n_s.at[0], n_r.at[s], sib).wait_recv()
        total = nrecv[0]
        for s in range(1, LAYERS):
            total = total + nrecv[s]
        no_ref[...] = jnp.sqrt(total + 1e-06)

    def decode(r):
        rows = jnp.concatenate(
            [
                acts[r, pl.ds(pl.multiple_of((1 - c) * 128, 128), 128), :],
                acts[r, pl.ds(pl.multiple_of(c * 128, 128), 128), :],
            ],
            axis=0,
        )

        @pl.loop(0, NSTEPS)
        def _(n):
            part = jnp.dot(
                rows, w[:, pl.ds(pl.multiple_of(n * NT, NT), NT)], preferred_element_type=F32
            )
            sibs[r, n] = part[:128].astype(BF16)
            opart[r, n] = part[128:]
            remote(sibs.at[r, n], sibr.at[r, n], cs_s.at[r, n], cs_r.at[r, n], sib).start()

    def chip_sum(r, q, n):
        rows = pl.ds(pl.multiple_of(q * PR, PR), PR)
        return opart[r, n, rows, :] + sibr[r, n, rows, :].astype(F32)

    def cols(n):
        return slice(n * NT, (n + 1) * NT)

    def y_copy(r, k):
        dev = yup if k in (0, 2, 3) else ydn
        return remote(ys.at[r, k], yr.at[r, k], cy_s.at[r, k], cy_r.at[r, k], dev)

    def y_wait(r, k):
        remote(yr.at[r, k], yr.at[r, k], cy_s.at[r, k], cy_r.at[r, k], sib).wait_recv()

    def c_a(r):
        for n in range(NSTEPS):
            remote(sibr.at[r, n], sibr.at[r, n], cs_s.at[r, n], cs_r.at[r, n], sib).wait_recv()
        for k, q in ((0, 2 * yo), (1, 2 * yo + 1), (3, 2 * yp + 1), (4, 2 * ym)):
            for n in range(NSTEPS):
                ys[r, k, :, cols(n)] = chip_sum(r, q, n).astype(BF16)
            y_copy(r, k).start()

    def c_b(r):
        for k, q, i in ((2, 2 * yp, 0), (5, 2 * ym + 1, 1)):
            y_wait(r, i)
            for n in range(NSTEPS):
                ys[r, k, :, cols(n)] = (
                    chip_sum(r, q, n) + yr[r, i, :, cols(n)].astype(F32)
                ).astype(BF16)
            y_copy(r, k).start()

    def z_copy(r):
        return remote(zs.at[r], zr.at[r], cz_s.at[r], cz_r.at[r], zpt)

    def c_c(r):
        for k in (2, 3, 4, 5):
            y_wait(r, k)
        for n in range(NSTEPS):
            other = chip_sum(r, 2 * y + 1 - zh, n)
            other = other + yr[r, 3 - zh, :, cols(n)].astype(F32)
            other = other + yr[r, 5 - zh, :, cols(n)].astype(F32)
            zs[r, :, cols(n)] = other.astype(BF16)
        z_copy(r).start()
        for n in range(NSTEPS):
            mine = chip_sum(r, 2 * y + zh, n)
            mine = mine + yr[r, 2 + zh, :, cols(n)].astype(F32)
            mine = mine + yr[r, 4 + zh, :, cols(n)].astype(F32)
            dkeep[:, cols(n)] = mine

    def c_d(r):
        ids = lax.broadcasted_iota(jnp.int32, (PR, ROWS), 0) + (2 * PR * t + PR * r)
        pick = (jnp.broadcast_to(order_ref[...], (PR, ROWS)) == ids).astype(F32).astype(BF16)
        wanted = jnp.dot(pick, tbuf[...].reshape(ROWS, D), preferred_element_type=F32)
        remote(zr.at[r], zr.at[r], cz_s.at[r], cz_r.at[r], sib).wait_recv()
        resid = (dkeep[...] + zr[r].astype(F32) + db_ref[...] - wanted) * SCALE
        rbuf[r, own_core] = resid.astype(BF16)
        ar[r].start()

    def f_copy(r, k, src, slot, dev):
        return remote(src, frecv.at[r, slot], f_s.at[r, k], f_r.at[r, slot], dev)

    def f_wait(r, slot):
        remote(frecv.at[r, slot], frecv.at[r, slot], f_s.at[r, 0], f_r.at[r, slot], sib).wait_recv()

    def f_sends(r, name):
        return {
            "a1": lambda: [f_copy(r, l, gb.at[r, l], l, xdn) for l in (0, 1)],
            "a2": lambda: [f_copy(r, l, gb.at[r, l], 2 + l, xup) for l in (0, 1)],
            "a3": lambda: [f_copy(r, 3, gb.at[r, 3], 4, xup), f_copy(r, 2, gb.at[r, 2], 4, xdn)],
            "b2": lambda: [f_copy(r, 3, gb.at[r, 3], 1, xdn)],
            "s2": lambda: [f_copy(r, 2, gb.at[r, 2], 0, xdn)],
            "b3": lambda: [f_copy(r, 4 + l, gb.at[r, 4 + l], l, xdn) for l in (0, 1)],
            "c3": lambda: [f_copy(r, l, gb.at[r, l], 2 + l, xup) for l in (0, 1)],
            "r0": lambda: [f_copy(r, 7, frecv.at[r, 4], 2, xup)],
        }[name]()

    def f_go(r, name, before=None):
        @pl.when(x == int(name[1]))
        def _():
            if before is not None:
                before()
            for cp in f_sends(r, name):
                cp.start()

    def grads(r, i):
        @pl.when(i <= x)
        def _():
            p = (i + x // 3) % 3 if i < 3 else 3
            g = lax.dot_general(
                rbuf[r].reshape(CR, D), w[pl.ds(pl.multiple_of(p * 2 * FS, 2 * FS), 2 * FS), :],
                NT_DIMS, preferred_element_type=F32,
            )

            @pl.when(x != i)
            def _():
                gb[r, 2 * p] = g[:, :FS].astype(BF16)
                gb[r, 2 * p + 1] = g[:, FS:].astype(BF16)

            @pl.when(x == i)
            def _():
                gown[r, 0] = g[:, :FS]
                gown[r, 1] = g[:, FS:] * zl.astype(F32)

        def add(pairs):
            def fn():
                for l, slot in pairs:
                    f_wait(r, slot)
                    gb[r, l] = (gb[r, l].astype(F32) + frecv[r, slot].astype(F32)).astype(BF16)

            return fn

        if i == 0:
            for name in ("a1", "a2", "a3"):
                f_go(r, name)
        if i == 1:
            f_go(r, "b2")
            f_go(r, "b3")
            f_go(r, "s2", add(((2, 4),)))
        if i == 2:
            f_go(r, "c3", add(((0, 2), (1, 3))))

    def f_relay(r):
        f_go(r, "r0", lambda: f_wait(r, 4))

    def f_zcopy(r):
        return remote(fzs.at[r], fzr.at[r], fz_s.at[r], fz_r.at[r], zpl)

    def f_fin1(r):
        for cond, adds in (
            (x == 0, ((0, 0), (1, 1), (0, 2), (1, 3))),
            (x == 1, ((0, 0), (1, 1), (1, 2))),
            (x == 2, ((0, 0), (1, 1))),
        ):

            @pl.when(cond)
            def _(adds=adds):
                for j, slot in adds:
                    f_wait(r, slot)
                    gown[r, j] = gown[r, j] + frecv[r, slot].astype(F32)

        fzs[r] = gown[r, 1 - zl].astype(BF16)
        f_zcopy(r).start()

    def f_fin2(r):
        remote(fzr.at[r], fzr.at[r], fz_s.at[r], fz_r.at[r], sib).wait_recv()
        total = gown[r, zl] + fzr[r].astype(F32)
        norm = no_ref[pl.ds(m, 1), :]
        grad = jnp.where(pre[r] > 0, total + norm * SCALE, 0.0)
        gl[r] = grad.astype(BF16)
        put(gl.at[r], go_hbm.at[pl.ds(r * CR, CR)], 6 + r)

    ax[0].start()
    ax[1].start()
    for k in range(3):
        local[k].wait()
    ax[0].relay1()
    ax[1].relay1()
    ax[0].relay2()
    ax[0].finish()
    encode(0)
    b_start(0)
    ax[1].relay2()
    ax[1].finish()
    encode(1)
    b_start(1)
    at.start()
    for r in range(CH):
        put(xbuf.at[r], xo_hbm.at[r], r)
    b_step1(0)
    b_step1(1)
    norms()
    local[3].wait()
    at.relay1()
    b_step2(0)
    b_step2(1)
    at.relay2()
    at.finish()
    b_finish(0)
    decode(0)
    put(acts.at[0], ao_hbm.at[0], 2)
    c_a(0)
    b_finish(1)
    decode(1)
    put(acts.at[1], ao_hbm.at[1], 3)
    c_b(0)
    c_a(1)
    c_c(0)
    c_d(0)
    c_b(1)
    ar[0].relay1()
    c_c(1)
    ar[0].relay2()
    c_d(1)
    norms_finish()
    ar[0].finish()
    put(rbuf.at[0], ro_hbm.at[0], 4)
    grads(0, 0)
    ar[1].relay1()
    grads(0, 1)
    ar[1].relay2()
    grads(0, 2)
    ar[1].finish()
    put(rbuf.at[1], ro_hbm.at[1], 5)
    grads(0, 3)
    f_relay(0)
    grads(1, 0)
    f_relay(1)
    grads(1, 1)
    f_fin1(0)
    grads(1, 2)
    grads(1, 3)
    f_fin2(0)
    f_fin1(1)
    f_fin2(1)

    for cp in sent:
        cp.wait_send()
    for r in range(CH):
        b_drain(r)
        for n in range(NSTEPS):
            remote(sibs.at[r, n], sibr.at[r, n], cs_s.at[r, n], cs_r.at[r, n], sib).wait_send()
        for k in range(6):
            y_copy(r, k).wait_send()
        z_copy(r).wait_send()
        for name in ("a1", "a2", "a3", "b2", "s2", "b3", "c3", "r0"):

            @pl.when(x == int(name[1]))
            def _(name=name):
                for cp in f_sends(r, name):
                    cp.wait_send()

        f_zcopy(r).wait_send()
    for k in range(1, LAYERS):
        norm_copy(k).wait_send()
    for cp in outs:
        cp.wait()


def run_main(x, tgt, order, we, eb, w, db):
    any_spec = pl.BlockSpec(memory_space=pl.ANY)
    vmem = pl.BlockSpec(memory_space=pltpu.VMEM)
    dma = pltpu.SemaphoreType.DMA
    return pl.pallas_call(
        main_kernel,
        out_shape=(
            jax.ShapeDtypeStruct((CH, TOKS, PR, D), BF16),
            jax.ShapeDtypeStruct((CH, CR, D), BF16),
            jax.ShapeDtypeStruct((CH, TOKS, PR, D), BF16),
            jax.ShapeDtypeStruct((CH * CR, FS), BF16),
            jax.ShapeDtypeStruct((LAYERS, FS), F32),
        ),
        in_specs=[any_spec, any_spec, vmem, any_spec, vmem, any_spec, vmem],
        out_specs=(any_spec, any_spec, any_spec, any_spec, vmem),
        scratch_shapes=[
            pltpu.VMEM((CH, TOKS, PR, D), BF16),
            pltpu.VMEM((TOKS, 2 * PR, D), BF16),
            pltpu.VMEM((CH, TOKS, PR, D), BF16),
            pltpu.VMEM((CH, CR, D), BF16),
            pltpu.VMEM((CH, CR, FS), BF16),
            pltpu.VMEM((CH, CR, FS), BF16),
            pltpu.VMEM((CH, CR, FS), F32),
            pltpu.VMEM((D, FS), BF16),
            pltpu.VMEM((LAYERS * FS, D), BF16),
            pltpu.VMEM((CH, NSTEPS, 128, NT), F32),
            pltpu.VMEM((CH, NSTEPS, 128, NT), BF16),
            pltpu.VMEM((CH, NSTEPS, 128, NT), BF16),
            pltpu.VMEM((CH, 6, PR, D), BF16),
            pltpu.VMEM((CH, 6, PR, D), BF16),
            pltpu.VMEM((CH, PR, D), BF16),
            pltpu.VMEM((CH, PR, D), BF16),
            pltpu.VMEM((PR, D), F32),
            pltpu.VMEM((CH, LAYERS, CR, FS), BF16),
            pltpu.VMEM((CH, 2, CR, FS), F32),
            pltpu.VMEM((CH, 5, CR, FS), BF16),
            pltpu.VMEM((CH, CR, FS), BF16),
            pltpu.VMEM((CH, CR, FS), BF16),
            pltpu.VMEM((8, 128), F32),
            pltpu.VMEM((LAYERS, LAYERS, FS), F32),
            pltpu.VMEM((CH, CR, FS), BF16),
            dma((4 + LAYERS,)), dma((8,)), dma((5, 15)), dma((5, TOKS)),
            dma((CH, 9)), dma((CH, 10)), dma((CH, NSTEPS)), dma((CH, NSTEPS)),
            dma((CH, 6)), dma((CH, 6)), dma((CH,)), dma((CH,)),
            dma((CH, 8)), dma((CH, 5)), dma((CH,)), dma((CH,)),
            dma((LAYERS,)), dma((LAYERS,)),
        ],
        compiler_params=pltpu.CompilerParams(
            collective_id=0, has_side_effects=True, vmem_limit_bytes=60 << 20
        ),
        name="window",
    )(x, tgt, order, we, eb, w, db)


def tail_kernel(m_ref, a_ref, r_ref, w_ref, n_ref, x_ref, g_ref, dw_ref, dwe_ref, fg_ref, og_ref):
    l = pl.program_id(0)
    m = m_ref[0]

    @pl.when(l == 0)
    def _():
        ones = jnp.ones((8, ROWS), BF16)
        g = g_ref[...]
        fg_ref[...] = jnp.dot(ones, g, preferred_element_type=F32)[0:1]
        og_ref[...] = jnp.dot(ones, r_ref[...], preferred_element_type=F32)[0:1]
        flipped = jnp.dot(g.T, x_ref[...], preferred_element_type=F32).astype(BF16)
        dwe_ref[...] = flipped.T

    @pl.when(l > m)
    def _():
        dw_ref[...] = jnp.zeros_like(dw_ref)

    @pl.when(l <= m)
    def _():
        at = a_ref[...].T
        sums = jnp.dot(at, jnp.ones((ROWS, 128), BF16), preferred_element_type=F32)
        pick = (lax.broadcasted_iota(jnp.int32, (LAYERS, 128), 0) == l).astype(F32)
        norm = lax.dot_general(
            n_ref[...], pick, TN_DIMS, preferred_element_type=F32, precision=lax.Precision.HIGHEST
        )
        factor = sums * SCALE / norm
        for n in range(4):
            cs = slice(n * 512, (n + 1) * 512)
            prod = jnp.dot(at, r_ref[:, cs], preferred_element_type=F32)
            fac = jnp.concatenate([factor] * 4, axis=1)
            dw_ref[0, :, cs] = (prod + fac * w_ref[0, :, cs].astype(F32)).astype(BF16)


def run_tail(m, acts, resid, w, norms, xs, gl):
    def fixed(shape):
        return pl.BlockSpec(shape, lambda l, m: (0,) * len(shape), pipeline_mode=pl.Buffered(1))

    return pl.pallas_call(
        tail_kernel,
        out_shape=(
            jax.ShapeDtypeStruct((LAYERS, FS, D), BF16),
            jax.ShapeDtypeStruct((D, FS), BF16),
            jax.ShapeDtypeStruct((1, FS), F32),
            jax.ShapeDtypeStruct((1, D), F32),
        ),
        grid_spec=pltpu.PrefetchScalarGridSpec(
            num_scalar_prefetch=1,
            grid=(LAYERS,),
            in_specs=[
                pl.BlockSpec((ROWS, FS), lambda l, m: (0, jnp.minimum(l, m[0]))),
                fixed((ROWS, D)),
                pl.BlockSpec((1, FS, D), lambda l, m: (jnp.minimum(l, m[0]), 0, 0)),
                fixed((LAYERS, FS)),
                fixed((ROWS, D)),
                fixed((ROWS, FS)),
            ],
            out_specs=(
                pl.BlockSpec((1, FS, D), lambda l, m: (l, 0, 0)),
                pl.BlockSpec((D, FS), lambda l, m: (0, 0)),
                pl.BlockSpec((1, FS), lambda l, m: (0, 0)),
                pl.BlockSpec((1, D), lambda l, m: (0, 0)),
            ),
        ),
        compiler_params=pltpu.CompilerParams(vmem_limit_bytes=50 << 20),
        name="weights",
    )(m, acts, resid, w, norms, xs, gl)


def on_device(x, tgt, order, we, eb, w, db):
    xs, acts, resid, gl, norms = run_main(x, tgt, order[None], we, eb, w, db)
    m = lax.axis_index("layer").astype(jnp.int32)[None]
    dw, dwe, fg, og = run_tail(
        m, acts.reshape(ROWS, D), resid.reshape(ROWS, D), w[0], norms, xs.reshape(ROWS, D), gl
    )
    return dwe[None], fg, dw[None], og


def solution(mesh):
    placed = (
        P("layer", "tok", None),
        P("layer", "tok", None),
        P(),
        P("layer", None, "tok"),
        P("layer", "tok"),
        P("layer", None, "tok", None),
        P("layer", None),
    )
    return jax.shard_map(
        on_device,
        mesh=mesh,
        in_specs=placed,
        out_specs=(
            P("layer", None, "tok"),
            P("layer", "tok"),
            P("layer", None, "tok", None),
            P("layer", None),
        ),
        check_vma=False,
    )
```

```python
import math

import jax
import jax.numpy as jnp
from jax import lax
from jax.experimental import pallas as pl
from jax.experimental.pallas import tpu as pltpu
from jax.sharding import PartitionSpec as P

MESH = pl.DeviceIdType.MESH
F32, BF16 = jnp.float32, jnp.bfloat16
NT_DIMS = (((1,), (1,)), ((), ()))
TN_DIMS = (((0,), (0,)), ((), ()))

LAYERS = 8
TOKS = 16
ROWS = 512
D = 2048
FS = 256
CH = 2
PR = 16
CR = TOKS * PR
NT = 512
NSTEPS = D // NT
HALVES = 2
HW = D // HALVES
HS = NSTEPS // HALVES
SCALE = 1.0 / math.sqrt(ROWS)


def main_kernel(
    x_hbm, t_hbm, order_ref, we_hbm, eb_ref, w_hbm, db_ref,
    xo, go, do, fo, oo,
    tbuf, rbuf, acts, pact, bact, pre, we, w,
    opart, sibs, sibr, ys, yr, zs, zr, dkeep, tpick,
    gb, gown, frecv, fzs, fzr, nrecv, no_ref, act_t,
    lsem, ag_s, ag_r, b_s, b_r, cs_s, cs_r, cy_s, cy_r, cz_s, cz_r,
    f_s, f_r, fz_s, fz_r, n_s, n_r,
):
    m, t = lax.axis_index("layer"), lax.axis_index("tok")
    x, zl = m // 2, m % 2
    y, zh, c = t // 4, (t // 2) % 2, t % 2
    yp, ym, yo = (y + 1) % 4, (y + 3) % 4, (y + 2) % 4
    xp, xm = (x + 1) % 4, (x + 3) % 4

    def tk(yy, zz, cc):
        return 4 * yy + 2 * zz + cc

    def by_core(yy, zz, cc):
        return 8 * cc + 2 * yy + zz

    sib, zpt = (m, tk(y, zh, 1 - c)), (m, tk(y, 1 - zh, c))
    yup, ydn = (m, tk(yp, zh, c)), (m, tk(ym, zh, c))
    xup, xdn = (2 * xp + zl, t), (2 * xm + zl, t)
    mp = m + 1 - 2 * zl
    zpl = (mp, t)

    def remote(src, dst, s, r, dev):
        return pltpu.make_async_remote_copy(
            src_ref=src, dst_ref=dst, send_sem=s, recv_sem=r, device_id=dev, device_id_type=MESH
        )

    local = []

    def fetch(src, dst, k):
        cp = pltpu.make_async_copy(src, dst, lsem.at[k])
        cp.start()
        local.append(cp)

    own_core = by_core(y, zh, c)
    for r in range(CH):
        fetch(x_hbm.at[0, pl.ds(r * PR, PR)], xo.at[r, own_core], r)
    fetch(we_hbm.at[0], we, 2)
    fetch(t_hbm.at[0], tbuf.at[t], 3)
    for l in range(LAYERS):
        fetch(w_hbm.at[0, l], w.at[pl.ds(l * FS, FS)], 4 + l)

    barrier = pltpu.get_barrier_semaphore()
    for dev in (sib, zpt, yup, ydn):
        pl.semaphore_signal(barrier, inc=1, device_id=dev, device_id_type=MESH)
    for k in range(1, LAYERS):
        pl.semaphore_signal(barrier, inc=1, device_id=((m + k) % LAYERS, t), device_id_type=MESH)
    pl.semaphore_wait(barrier, 4 + LAYERS - 1)

    class Gather:
        def __init__(self, inst, at, many, slot):
            self.inst, self.at, self.many, self.slot = inst, at, many, slot

        def send(self, slot, dev, sem):
            remote(self.at(slot), self.at(slot), ag_s.at[self.inst], ag_r.at[self.inst, sem], dev).start()

        def wait(self, slot, sem):
            remote(self.at(slot), self.at(slot), ag_s.at[self.inst], ag_r.at[self.inst, sem], sib).wait_recv()

        def to_sib(self, yy, zz):
            shared = self.slot is by_core
            self.send(self.slot(yy, zz, c), sib, 8 if shared else 8 + 2 * yy + zz)

        def to(self, yy, zz, *devs):
            for dev in devs:
                self.send(self.slot(yy, zz, c), dev, 2 * yy + zz)

        def take(self, yy, zz):
            self.wait(self.slot(yy, zz, c), 2 * yy + zz)

        def start(self):
            self.to(y, zh, zpt, yup, ydn)
            self.to_sib(y, zh)

        def relay_z(self):
            self.take(y, 1 - zh)
            self.to(y, 1 - zh, yup, ydn)
            self.to_sib(y, 1 - zh)

        def relay_y(self):
            self.take(ym, zh)
            self.to(ym, zh, yup)
            self.to_sib(ym, zh)
            self.take(yp, zh)
            self.to_sib(yp, zh)

        def relay_zy(self):
            self.take(yp, 1 - zh)
            self.to(yp, 1 - zh, ydn)
            self.to_sib(yp, 1 - zh)
            self.take(ym, 1 - zh)
            self.to_sib(ym, 1 - zh)

        def far_y(self):
            self.take(yo, zh)
            self.to_sib(yo, zh)

        def finish(self):
            self.take(yo, 1 - zh)
            self.to_sib(yo, 1 - zh)
            if self.slot is by_core:
                ref = self.many(8 * (1 - c), 8)
                remote(ref, ref, ag_s.at[self.inst], ag_r.at[self.inst, 8], sib).wait_recv()
            else:
                for yy in range(4):
                    for zz in range(2):
                        self.wait(self.slot(yy, zz, 1 - c), 8 + 2 * yy + zz)

        def drain(self):
            ref = self.many(0, 15)
            remote(ref, ref, ag_s.at[self.inst], ag_r.at[self.inst, 0], sib).wait_send()

    def half(h):
        return slice(h * HW, (h + 1) * HW)

    ax = [
        Gather(
            r, (lambda s, r=r: xo.at[r, s]), (lambda s, n, r=r: xo.at[r, pl.ds(s, n)]), by_core
        )
        for r in range(CH)
    ]
    at = Gather(2, (lambda s: tbuf.at[s]), (lambda s, n: tbuf.at[pl.ds(s, n)]), tk)
    ar = [
        [
            Gather(
                3 + HALVES * r + h,
                (lambda s, r=r, h=h: rbuf.at[r, s, :, half(h)]),
                (lambda s, n, r=r, h=h: rbuf.at[r, pl.ds(s, n), :, half(h)]),
                by_core,
            )
            for h in range(HALVES)
        ]
        for r in range(CH)
    ]

    def encode(r):
        rows = xo[r].reshape(CR, D)
        value = jnp.dot(rows, we[...], preferred_element_type=F32) + eb_ref[...]
        pre[r] = value
        acts[r, :, pl.ds(pl.multiple_of(m * FS, FS), FS)] = jnp.maximum(value, 0.0).astype(BF16)

    def act_at(r, l):
        return acts.at[r, :, pl.ds(pl.multiple_of(l * FS, FS), FS)]

    def b_copy(r, k, src, dst, slot, dev):
        return remote(src, dst, b_s.at[r, k], b_r.at[r, slot], dev)

    def b_wait(r, l):
        b_copy(r, 0, act_at(r, l), act_at(r, l), l, sib).wait_recv()

    def b_own(r):
        return [
            (None, b_copy(r, 0, act_at(r, m), pact.at[r], 8, zpl)),
            (x < 3, b_copy(r, 1, act_at(r, m), act_at(r, m), m, xup)),
            (x == 0, b_copy(r, 2, act_at(r, m), act_at(r, m), m, xdn)),
            (m == 3, b_copy(r, 3, act_at(r, m), bact.at[r], 9, xdn)),
        ]

    def b_partner(r):
        return [
            (x < 3, b_copy(r, 4, pact.at[r], act_at(r, mp), mp, xup)),
            (x == 0, b_copy(r, 5, pact.at[r], act_at(r, mp), mp, xdn)),
            (m == 2, b_copy(r, 6, pact.at[r], bact.at[r], 9, xdn)),
        ]

    def b_relay_a(r):
        return [
            (m == 1, 9, b_copy(r, 7, bact.at[r], act_at(r, 3), 3, xdn)),
            (m == 4, 2, b_copy(r, 7, act_at(r, 2), act_at(r, 2), 2, xup)),
            (x == 3, zl, b_copy(r, 7, act_at(r, zl), act_at(r, zl), zl, xdn)),
        ]

    def b_relay_b(r):
        o = 1 - zl
        return [
            (m == 0, 9, b_copy(r, 7, bact.at[r], act_at(r, 3), 3, xdn)),
            (m == 5, 2, b_copy(r, 7, act_at(r, 2), act_at(r, 2), 2, xup)),
            (x == 3, o, b_copy(r, 8, act_at(r, o), act_at(r, o), o, xdn)),
        ]

    def when(cond, fn):
        if cond is None:
            fn()
        else:
            pl.when(cond)(fn)

    def b_start(r):
        for cond, cp in b_own(r):
            when(cond, cp.start)

    def b_step1(r):
        remote(pact.at[r], pact.at[r], b_s.at[r, 0], b_r.at[r, 8], sib).wait_recv()
        for cond, cp in b_partner(r):
            when(cond, cp.start)

        @pl.when(zl == 1)
        def _():
            acts[r, :, pl.ds(pl.multiple_of(mp * FS, FS), FS)] = pact[r]

    def b_pass(r, relays):
        for cond, slot, cp in relays(r):

            def go(slot=slot, cp=cp):
                if isinstance(slot, int) and slot == 9:
                    remote(bact.at[r], bact.at[r], b_s.at[r, 0], b_r.at[r, 9], sib).wait_recv()
                else:
                    b_wait(r, slot)
                cp.start()

            when(cond, go)

    def b_finish(r):
        for cond, slots in ((x == 1, (0, 1)), (x == 2, (0, 1, 3)), (x == 3, (2, 3, 4, 5))):
            when(cond, lambda slots=slots: [b_wait(r, l) for l in slots] and None)

    def b_drain(r):
        for cond, cp in b_own(r) + b_partner(r):
            when(cond, cp.wait_send)
        for cond, _, cp in b_relay_a(r) + b_relay_b(r):
            when(cond, cp.wait_send)

    def clear():
        for l in range(1, LAYERS):

            @pl.when(l > m)
            def _(l=l):
                acts[:, :, l * FS : (l + 1) * FS] = jnp.zeros((CH, CR, FS), BF16)

    def norm_copy(k):
        return remote(nrecv.at[m], nrecv.at[m], n_s.at[k], n_r.at[m], ((m + k) % LAYERS, t))

    def norms(lo, hi):
        for k in range(lo, hi):
            local[4 + k].wait()

        @pl.loop(lo, hi)
        def _(l):
            part = jnp.zeros((FS, 128), F32)
            for j in range(D // 128):
                v = w[pl.ds(pl.multiple_of(l * FS, FS), FS), j * 128 : (j + 1) * 128].astype(F32)
                part = part + v * v
            row = lax.dot_general(
                jnp.ones((8, 128), F32), part, NT_DIMS,
                preferred_element_type=F32, precision=lax.Precision.HIGHEST,
            )
            keep = jnp.where(l <= m, 1.0, 0.0).astype(F32)
            nrecv[m, pl.ds(l, 1), :] = row[0:1] * keep

        if hi == LAYERS:
            for k in range(1, LAYERS):
                norm_copy(k).start()

    def norms_finish():
        for k in range(1, LAYERS):
            s = (m + k) % LAYERS
            remote(nrecv.at[s], nrecv.at[s], n_s.at[0], n_r.at[s], sib).wait_recv()
        total = nrecv[0]
        for s in range(1, LAYERS):
            total = total + nrecv[s]
        no_ref[...] = jnp.sqrt(total + 1e-06)

    def decode(r, h):
        rows = jnp.concatenate(
            [
                acts[r, pl.ds(pl.multiple_of((1 - c) * 128, 128), 128), :],
                acts[r, pl.ds(pl.multiple_of(c * 128, 128), 128), :],
            ],
            axis=0,
        )

        @pl.loop(h * HS, (h + 1) * HS)
        def _(n):
            part = jnp.dot(
                rows, w[:, pl.ds(pl.multiple_of(n * NT, NT), NT)], preferred_element_type=F32
            )
            sibs[r, n] = part[:128].astype(BF16)
            opart[r, n] = part[128:]
            remote(sibs.at[r, n], sibr.at[r, n], cs_s.at[r, n], cs_r.at[r, n], sib).start()

    def cols(n):
        return slice(n * NT, (n + 1) * NT)

    def steps(h):
        return range(h * HS, (h + 1) * HS)

    def chip_sum(r, q, n):
        rows = pl.ds(pl.multiple_of(q * PR, PR), PR)
        return opart[r, n, rows, :] + sibr[r, n, rows, :].astype(F32)

    def y_copy(r, h, k):
        dev = yup if k in (0, 2, 3) else ydn
        src, dst = ys.at[r, k, :, half(h)], yr.at[r, k, :, half(h)]
        return remote(src, dst, cy_s.at[r, h], cy_r.at[r, h, k], dev)

    def y_wait(r, h, k):
        y_copy(r, h, k).wait_recv()

    def c_a(r, h):
        for n in steps(h):
            remote(sibr.at[r, n], sibr.at[r, n], cs_s.at[r, n], cs_r.at[r, n], sib).wait_recv()
        for k, q in ((0, 2 * yo), (1, 2 * yo + 1), (3, 2 * yp + 1), (4, 2 * ym)):
            for n in steps(h):
                ys[r, k, :, cols(n)] = chip_sum(r, q, n).astype(BF16)
            y_copy(r, h, k).start()

    def c_b(r, h):
        for k, q, i in ((2, 2 * yp, 0), (5, 2 * ym + 1, 1)):
            y_wait(r, h, i)
            for n in steps(h):
                ys[r, k, :, cols(n)] = (
                    chip_sum(r, q, n) + yr[r, i, :, cols(n)].astype(F32)
                ).astype(BF16)
            y_copy(r, h, k).start()

    def z_copy(r, h):
        src, dst = zs.at[r, :, half(h)], zr.at[r, :, half(h)]
        return remote(src, dst, cz_s.at[r, h], cz_r.at[r, h], zpt)

    def c_c(r, h):
        for k in (2, 3, 4, 5):
            y_wait(r, h, k)
        for n in steps(h):
            other = chip_sum(r, 2 * y + 1 - zh, n)
            other = other + yr[r, 3 - zh, :, cols(n)].astype(F32)
            other = other + yr[r, 5 - zh, :, cols(n)].astype(F32)
            zs[r, :, cols(n)] = other.astype(BF16)
        z_copy(r, h).start()
        for n in steps(h):
            mine = chip_sum(r, 2 * y + zh, n)
            mine = mine + yr[r, 2 + zh, :, cols(n)].astype(F32)
            mine = mine + yr[r, 4 + zh, :, cols(n)].astype(F32)
            dkeep[r, :, cols(n)] = mine

    def pick_targets():
        for r in range(CH):
            ids = lax.broadcasted_iota(jnp.int32, (PR, ROWS), 0) + (2 * PR * t + PR * r)
            pick = (jnp.broadcast_to(order_ref[...], (PR, ROWS)) == ids).astype(F32).astype(BF16)
            wanted = jnp.dot(pick, tbuf[...].reshape(ROWS, D), preferred_element_type=F32)
            tpick[r] = db_ref[...] - wanted

    def c_d(r, h):
        z_copy(r, h).wait_recv()
        resid = (dkeep[r, :, half(h)] + zr[r, :, half(h)].astype(F32) + tpick[r, :, half(h)]) * SCALE
        rbuf[r, own_core, :, half(h)] = resid.astype(BF16)
        ar[r][h].start()

    def f_copy(r, k, src, slot, dev):
        return remote(src, frecv.at[r, slot], f_s.at[r, k], f_r.at[r, slot], dev)

    def f_wait(r, slot):
        remote(frecv.at[r, slot], frecv.at[r, slot], f_s.at[r, 0], f_r.at[r, slot], sib).wait_recv()

    def f_sends(r, name):
        return {
            "a1": lambda: [f_copy(r, 0, gb.at[r, 0], 0, xdn)],
            "s1": lambda: [f_copy(r, 1, gb.at[r, 1], 1, xdn)],
            "a2": lambda: [
                f_copy(r, 0, gb.at[r, 0], 2, xup),
                f_copy(r, 1, gb.at[r, 1], 4, xdn),
            ],
            "a3": lambda: [f_copy(r, 3, gb.at[r, 3], 4, xup), f_copy(r, 2, gb.at[r, 2], 4, xdn)],
            "b2": lambda: [f_copy(r, 3, gb.at[r, 3], 1, xdn)],
            "s2": lambda: [f_copy(r, 2, gb.at[r, 2], 0, xdn)],
            "b3": lambda: [f_copy(r, 4 + l, gb.at[r, 4 + l], l, xdn) for l in (0, 1)],
            "c3": lambda: [f_copy(r, 1, gb.at[r, 1], 3, xup)],
            "s3": lambda: [f_copy(r, 0, gb.at[r, 0], 2, xup)],
            "r0": lambda: [f_copy(r, 7, frecv.at[r, 4], 2, xup)],
        }[name]()

    def f_go(r, name, before=None):
        @pl.when(x == int(name[1]))
        def _():
            if before is not None:
                before()
            for cp in f_sends(r, name):
                cp.start()

    def grads(r, i):
        @pl.when(i <= x)
        def _():
            p = (i + x // 3) % 3 if i < 3 else 3
            g = lax.dot_general(
                rbuf[r].reshape(CR, D), w[pl.ds(pl.multiple_of(p * 2 * FS, 2 * FS), 2 * FS), :],
                NT_DIMS, preferred_element_type=F32,
            )

            @pl.when(x != i)
            def _():
                gb[r, 2 * p] = g[:, :FS].astype(BF16)
                gb[r, 2 * p + 1] = g[:, FS:].astype(BF16)

            @pl.when(x == i)
            def _():
                gown[r, 0] = g[:, :FS]
                gown[r, 1] = g[:, FS:] * zl.astype(F32)

        def add(pairs):
            def fn():
                for l, slot in pairs:
                    f_wait(r, slot)
                    gb[r, l] = (gb[r, l].astype(F32) + frecv[r, slot].astype(F32)).astype(BF16)

            return fn

        if i == 0:
            for name in ("a1", "a2", "a3"):
                f_go(r, name)
        if i == 1:
            f_go(r, "b2")
            f_go(r, "b3")
        if i == 2:
            f_go(r, "c3")

    def f_add(r):
        def add(l, slot):
            def fn():
                f_wait(r, slot)
                gb[r, l] = (gb[r, l].astype(F32) + frecv[r, slot].astype(F32)).astype(BF16)

            return fn

        f_go(r, "s1", add(1, 4))
        f_go(r, "s2", add(2, 4))
        f_go(r, "s3", add(0, 2))

    def f_relay(r):
        f_go(r, "r0", lambda: f_wait(r, 4))

    def f_zcopy(r):
        return remote(fzs.at[r], fzr.at[r], fz_s.at[r], fz_r.at[r], zpl)

    def f_fin1(r):
        for cond, adds in (
            (x == 0, ((0, 0), (1, 1), (0, 2), (1, 3))),
            (x == 1, ((0, 0), (1, 1), (1, 2))),
            (x == 2, ((0, 0), (1, 1))),
        ):

            @pl.when(cond)
            def _(adds=adds):
                for j, slot in adds:
                    f_wait(r, slot)
                    gown[r, j] = gown[r, j] + frecv[r, slot].astype(F32)

        fzs[r] = gown[r, 1 - zl].astype(BF16)
        f_zcopy(r).start()

    def f_fin2(r):
        remote(fzr.at[r], fzr.at[r], fz_s.at[r], fz_r.at[r], sib).wait_recv()
        total = gown[r, zl] + fzr[r].astype(F32)
        norm = no_ref[pl.ds(m, 1), :]
        grad = jnp.where(pre[r] > 0, total + norm * SCALE, 0.0)
        go[r] = grad.astype(BF16)
        fsum = jnp.sum(grad, axis=0, keepdims=True)
        fo[...] = fsum if r == 0 else fo[...] + fsum

    def flip(r):
        @pl.loop(0, LAYERS)
        def _(l):
            block = acts[r, :, pl.ds(pl.multiple_of(l * FS, FS), FS)]
            act_t[l, :, r * CR : (r + 1) * CR] = block.T

    def dec_zero():
        for l in range(1, LAYERS):

            @pl.when(l > m)
            def _(l=l):
                do[l] = jnp.zeros((FS, D), BF16)

    def dec_grads(lo, hi):
        @pl.loop(lo, hi)
        def _(l):
            @pl.when(l <= m)
            def _():
                a_t = act_t[l]
                sums = jnp.dot(a_t, jnp.ones((ROWS, 128), BF16), preferred_element_type=F32)
                pick = (lax.broadcasted_iota(jnp.int32, (LAYERS, 128), 0) == l).astype(F32)
                norm = lax.dot_general(
                    no_ref[...], pick, TN_DIMS,
                    preferred_element_type=F32, precision=lax.Precision.HIGHEST,
                )
                factor = jnp.concatenate([sums * SCALE / norm] * 4, axis=1)
                rows = pl.ds(pl.multiple_of(l * FS, FS), FS)
                for n in range(NSTEPS):
                    part = jnp.dot(
                        a_t, rbuf[:, :, :, cols(n)].reshape(ROWS, NT), preferred_element_type=F32
                    )
                    do[l, :, cols(n)] = (part + factor * w[rows, cols(n)].astype(F32)).astype(BF16)

    def out_sum():
        ones = jnp.ones((8, ROWS), BF16)
        oo[...] = jnp.dot(ones, rbuf[...].reshape(ROWS, D), preferred_element_type=F32)[0:1]

    for k in range(2):
        local[k].wait()
    ax[0].start()
    clear()
    dec_zero()
    ax[0].relay_z()
    ax[0].relay_y()
    ax[1].start()
    norms(0, 4)
    ax[0].relay_zy()
    ax[0].far_y()
    ax[1].relay_z()
    ax[1].relay_y()
    local[2].wait()
    local[3].wait()
    ax[0].finish()
    encode(0)
    b_start(0)
    ax[1].relay_zy()
    ax[1].far_y()
    ax[1].finish()
    encode(1)
    b_step1(0)
    b_start(1)
    at.start()
    b_pass(0, b_relay_a)
    norms(4, 8)
    b_pass(0, b_relay_b)
    at.relay_z()
    at.relay_y()
    b_step1(1)
    b_pass(1, b_relay_a)
    b_finish(0)
    decode(0, 0)
    b_pass(1, b_relay_b)
    at.relay_zy()
    at.far_y()
    c_a(0, 0)
    decode(0, 1)
    c_a(0, 1)
    c_b(0, 0)
    at.finish()
    pick_targets()
    b_finish(1)
    c_b(0, 1)
    c_c(0, 0)
    decode(1, 0)
    c_a(1, 0)
    c_c(0, 1)
    decode(1, 1)
    c_a(1, 1)
    c_d(0, 0)
    c_b(1, 0)
    c_d(0, 1)
    c_b(1, 1)
    ar[0][0].relay_z()
    ar[0][0].relay_y()
    c_c(1, 0)
    ar[0][1].relay_z()
    ar[0][1].relay_y()
    c_c(1, 1)
    ar[0][0].relay_zy()
    ar[0][0].far_y()
    c_d(1, 0)
    ar[0][1].relay_zy()
    ar[0][1].far_y()
    c_d(1, 1)
    flip(0)
    ar[0][0].finish()
    ar[0][1].finish()
    ar[1][0].relay_z()
    ar[1][0].relay_y()
    grads(0, 0)
    ar[1][1].relay_z()
    ar[1][1].relay_y()
    grads(0, 1)
    ar[1][0].relay_zy()
    ar[1][0].far_y()
    grads(0, 2)
    ar[1][1].relay_zy()
    ar[1][1].far_y()
    grads(0, 3)
    flip(1)
    norms_finish()
    ar[1][0].finish()
    ar[1][1].finish()
    f_add(0)
    grads(1, 0)
    grads(1, 1)
    grads(1, 2)
    f_relay(0)
    grads(1, 3)
    out_sum()
    dec_grads(0, 4)
    f_add(1)
    f_relay(1)
    f_fin1(0)
    dec_grads(4, 8)
    f_fin2(0)
    f_fin1(1)
    f_fin2(1)

    for g in ax + [at] + ar[0] + ar[1]:
        g.drain()
    for r in range(CH):
        b_drain(r)
        for n in range(NSTEPS):
            remote(sibs.at[r, n], sibr.at[r, n], cs_s.at[r, n], cs_r.at[r, n], sib).wait_send()
        for h in range(HALVES):
            ref = ys.at[r, :, :, half(h)]
            remote(ref, ref, cy_s.at[r, h], cy_r.at[r, h, 0], sib).wait_send()
            z_copy(r, h).wait_send()
        for name in ("a1", "s1", "a2", "a3", "b2", "s2", "b3", "c3", "s3", "r0"):

            @pl.when(x == int(name[1]))
            def _(name=name):
                for cp in f_sends(r, name):
                    cp.wait_send()

        f_zcopy(r).wait_send()
    for k in range(1, LAYERS):
        norm_copy(k).wait_send()


def run_main(x, tgt, order, we, eb, w, db):
    any_spec = pl.BlockSpec(memory_space=pl.ANY)
    vmem = pl.BlockSpec(memory_space=pltpu.VMEM)
    dma = pltpu.SemaphoreType.DMA
    return pl.pallas_call(
        main_kernel,
        out_shape=(
            pltpu.VMEM((CH, TOKS, PR, D), BF16),
            pltpu.VMEM((CH, CR, FS), BF16),
            pltpu.VMEM((LAYERS, FS, D), BF16),
            pltpu.VMEM((1, FS), F32),
            pltpu.VMEM((1, D), F32),
        ),
        in_specs=[any_spec, any_spec, vmem, any_spec, vmem, any_spec, vmem],
        out_specs=(vmem,) * 5,
        scratch_shapes=[
            pltpu.VMEM((TOKS, 2 * PR, D), BF16),
            pltpu.VMEM((CH, TOKS, PR, D), BF16),
            pltpu.VMEM((CH, CR, D), BF16),
            pltpu.VMEM((CH, CR, FS), BF16),
            pltpu.VMEM((CH, CR, FS), BF16),
            pltpu.VMEM((CH, CR, FS), F32),
            pltpu.VMEM((D, FS), BF16),
            pltpu.VMEM((LAYERS * FS, D), BF16),
            pltpu.VMEM((CH, NSTEPS, 128, NT), F32),
            pltpu.VMEM((CH, NSTEPS, 128, NT), BF16),
            pltpu.VMEM((CH, NSTEPS, 128, NT), BF16),
            pltpu.VMEM((CH, 6, PR, D), BF16),
            pltpu.VMEM((CH, 6, PR, D), BF16),
            pltpu.VMEM((CH, PR, D), BF16),
            pltpu.VMEM((CH, PR, D), BF16),
            pltpu.VMEM((CH, PR, D), F32),
            pltpu.VMEM((CH, PR, D), F32),
            pltpu.VMEM((CH, LAYERS, CR, FS), BF16),
            pltpu.VMEM((CH, 2, CR, FS), F32),
            pltpu.VMEM((CH, 5, CR, FS), BF16),
            pltpu.VMEM((CH, CR, FS), BF16),
            pltpu.VMEM((CH, CR, FS), BF16),
            pltpu.VMEM((LAYERS, LAYERS, FS), F32),
            pltpu.VMEM((LAYERS, FS), F32),
            pltpu.VMEM((LAYERS, FS, ROWS), BF16),
            dma((4 + LAYERS,)), dma((3 + CH * HALVES,)), dma((3 + CH * HALVES, TOKS)),
            dma((CH, 9)), dma((CH, 10)), dma((CH, NSTEPS)), dma((CH, NSTEPS)),
            dma((CH, HALVES)), dma((CH, HALVES, 6)), dma((CH, HALVES)), dma((CH, HALVES)),
            dma((CH, 8)), dma((CH, 5)), dma((CH,)), dma((CH,)),
            dma((LAYERS,)), dma((LAYERS,)),
        ],
        compiler_params=pltpu.CompilerParams(
            collective_id=0, has_side_effects=True, vmem_limit_bytes=46 << 20
        ),
        name="window",
    )(x, tgt, order, we, eb, w, db)


def tail_kernel(x_ref, g_ref, d_ref, f_ref, o_ref, dw_hbm, dwe_hbm, fg_hbm, og_hbm, enc, sems):
    copies = [
        pltpu.make_async_copy(d_ref, dw_hbm.at[0], sems.at[0]),
        pltpu.make_async_copy(f_ref, fg_hbm, sems.at[2]),
        pltpu.make_async_copy(o_ref, og_hbm, sems.at[3]),
    ]
    for cp in copies:
        cp.start()
    g = g_ref[...].reshape(ROWS, FS).T
    for n in range(NSTEPS):
        cs = slice(n * NT, (n + 1) * NT)
        part = jnp.dot(g, x_ref[:, :, :, cs].reshape(ROWS, NT), preferred_element_type=F32)
        enc[cs, :] = part.astype(BF16).T
    copies.append(pltpu.make_async_copy(enc, dwe_hbm.at[0], sems.at[1]))
    copies[-1].start()
    for cp in copies:
        cp.wait()


def run_tail(xs, gl, dec, fg, og):
    any_spec = pl.BlockSpec(memory_space=pl.ANY)
    vmem = pl.BlockSpec(memory_space=pltpu.VMEM)
    return pl.pallas_call(
        tail_kernel,
        out_shape=(
            jax.ShapeDtypeStruct((1, LAYERS, FS, D), BF16),
            jax.ShapeDtypeStruct((1, D, FS), BF16),
            jax.ShapeDtypeStruct((1, FS), F32),
            jax.ShapeDtypeStruct((1, D), F32),
        ),
        in_specs=[vmem] * 5,
        out_specs=(any_spec,) * 4,
        scratch_shapes=[pltpu.VMEM((D, FS), BF16), pltpu.SemaphoreType.DMA((4,))],
        compiler_params=pltpu.CompilerParams(vmem_limit_bytes=20 << 20),
        name="weights",
    )(xs, gl, dec, fg, og)


def on_device(x, tgt, order, we, eb, w, db):
    xs, gl, dec, fg, og = run_main(x, tgt, order[None], we, eb, w, db)
    dw, dwe, fg, og = run_tail(xs, gl, dec, fg, og)
    return dwe, fg, dw, og


def solution(mesh):
    placed = (
        P("layer", "tok", None),
        P("layer", "tok", None),
        P(),
        P("layer", None, "tok"),
        P("layer", "tok"),
        P("layer", None, "tok", None),
        P("layer", None),
    )
    return jax.shard_map(
        on_device,
        mesh=mesh,
        in_specs=placed,
        out_specs=(
            P("layer", None, "tok"),
            P("layer", "tok"),
            P("layer", None, "tok", None),
            P("layer", None),
        ),
        check_vma=False,
    )
```

```python
import math

import jax
import jax.numpy as jnp
from jax import lax
from jax.experimental import pallas as pl
from jax.experimental.pallas import tpu as pltpu
from jax.sharding import PartitionSpec as P

MESH = pl.DeviceIdType.MESH
F32, BF16 = jnp.float32, jnp.bfloat16
NT_DIMS = (((1,), (1,)), ((), ()))
TN_DIMS = (((0,), (0,)), ((), ()))

LAYERS = 8
TOKS = 16
ROWS = 512
D = 2048
FS = 256
CH = 2
PR = 16
CR = TOKS * PR
NT = 512
NSTEPS = D // NT
HALVES = 2
HW = D // HALVES
HS = NSTEPS // HALVES
SCALE = 1.0 / math.sqrt(ROWS)


def main_kernel(
    x_hbm, t_hbm, order_ref, we_hbm, eb_ref, w_hbm, db_ref,
    xo, go, do, fo, oo,
    tbuf, rbuf, acts, pact, bact, pre, we, w,
    opart, sibs, sibr, ys, yr, hit,
    gb, gown, frecv, fzs, fzr, nrecv, no_ref, act_t,
    lsem, ag_s, ag_r, b_s, b_r, cs_s, cs_r, cy_s, cy_r,
    f_s, f_r, fz_s, fz_r, n_s, n_r,
):
    m, t = lax.axis_index("layer"), lax.axis_index("tok")
    x, zl = m // 2, m % 2
    y, zh, c = t // 4, (t // 2) % 2, t % 2
    xp, xm = (x + 1) % 4, (x + 3) % 4

    def tk(yy, zz, cc):
        return 4 * yy + 2 * zz + cc

    sib = (m, tk(y, zh, 1 - c))
    others = [
        ((y + dy) % 4, (zh + dz) % 2) for dy, dz in ((2, 1), (1, 1), (3, 1), (2, 0), (0, 1), (1, 0), (3, 0))
    ]
    peers = [(2 * yy + zz, (m, tk(yy, zz, c))) for yy, zz in others]
    place = 2 * y + zh
    xup, xdn = (2 * xp + zl, t), (2 * xm + zl, t)
    mp = m + 1 - 2 * zl
    zpl = (mp, t)

    def remote(src, dst, s, r, dev):
        return pltpu.make_async_remote_copy(
            src_ref=src, dst_ref=dst, send_sem=s, recv_sem=r, device_id=dev, device_id_type=MESH
        )

    local = []

    def fetch(src, dst, k):
        cp = pltpu.make_async_copy(src, dst, lsem.at[k])
        cp.start()
        local.append(cp)

    own_core = 8 * c + place
    for r in range(CH):
        fetch(x_hbm.at[0, pl.ds(r * PR, PR)], xo.at[r, own_core], r)
    fetch(we_hbm.at[0], we, 2)
    fetch(t_hbm.at[0], tbuf.at[pl.ds(0, 2 * PR)], 3)
    for l in range(LAYERS):
        fetch(w_hbm.at[0, l], w.at[pl.ds(l * FS, FS)], 4 + l)

    barrier = pltpu.get_barrier_semaphore()
    for dev in [sib] + [dev for _, dev in peers]:
        pl.semaphore_signal(barrier, inc=1, device_id=dev, device_id_type=MESH)
    for k in range(1, LAYERS):
        pl.semaphore_signal(barrier, inc=1, device_id=((m + k) % LAYERS, t), device_id_type=MESH)
    pl.semaphore_wait(barrier, 8 + LAYERS - 1)

    class Gather:
        def __init__(self, inst, at):
            self.inst, self.at = inst, at

        def copy(self, core, first, number, k, dev):
            ref = self.at(core, first, number)
            return remote(ref, ref, ag_s.at[self.inst, k], ag_r.at[self.inst, k], dev)

        def start(self):
            for _, dev in peers:
                self.copy(c, place, 1, 0, dev).start()

        def sent(self):
            self.copy(c, 0, 7, 0, sib).wait_send()

        def take(self):
            self.copy(c, 0, 7, 0, sib).wait_recv()
            self.copy(c, 0, 8, 1, sib).start()

        def finish(self):
            self.copy(1 - c, 0, 8, 1, sib).wait_recv()

        def drain(self):
            self.copy(c, 0, 8, 1, sib).wait_send()

    def half(h):
        return slice(h * HW, (h + 1) * HW)

    ax = [Gather(r, lambda cc, f, n, r=r: xo.at[r, pl.ds(8 * cc + f, n)]) for r in range(CH)]
    ar = [
        [
            Gather(
                CH + HALVES * r + h,
                lambda cc, f, n, r=r, h=h: rbuf.at[r, pl.ds(8 * cc + f, n), :, half(h)],
            )
            for h in range(HALVES)
        ]
        for r in range(CH)
    ]

    def encode(r):
        rows = xo[r].reshape(CR, D)
        value = jnp.dot(rows, we[...], preferred_element_type=F32) + eb_ref[...]
        pre[r] = value
        acts[r, :, pl.ds(pl.multiple_of(m * FS, FS), FS)] = jnp.maximum(value, 0.0).astype(BF16)

    def act_at(r, l):
        return acts.at[r, :, pl.ds(pl.multiple_of(l * FS, FS), FS)]

    def b_copy(r, k, src, dst, slot, dev):
        return remote(src, dst, b_s.at[r, k], b_r.at[r, slot], dev)

    def b_wait(r, l):
        b_copy(r, 0, act_at(r, l), act_at(r, l), l, sib).wait_recv()

    def b_own(r):
        return [
            (None, b_copy(r, 0, act_at(r, m), pact.at[r], 8, zpl)),
            (x < 3, b_copy(r, 1, act_at(r, m), act_at(r, m), m, xup)),
            (x == 0, b_copy(r, 2, act_at(r, m), act_at(r, m), m, xdn)),
            (m == 3, b_copy(r, 3, act_at(r, m), bact.at[r], 9, xdn)),
        ]

    def b_partner(r):
        return [
            (x < 3, b_copy(r, 4, pact.at[r], act_at(r, mp), mp, xup)),
            (x == 0, b_copy(r, 5, pact.at[r], act_at(r, mp), mp, xdn)),
            (m == 2, b_copy(r, 6, pact.at[r], bact.at[r], 9, xdn)),
        ]

    def b_relay_a(r):
        return [
            (m == 1, 9, b_copy(r, 7, bact.at[r], act_at(r, 3), 3, xdn)),
            (m == 4, 2, b_copy(r, 7, act_at(r, 2), act_at(r, 2), 2, xup)),
            (x == 3, zl, b_copy(r, 7, act_at(r, zl), act_at(r, zl), zl, xdn)),
        ]

    def b_relay_b(r):
        o = 1 - zl
        return [
            (m == 0, 9, b_copy(r, 7, bact.at[r], act_at(r, 3), 3, xdn)),
            (m == 5, 2, b_copy(r, 7, act_at(r, 2), act_at(r, 2), 2, xup)),
            (x == 3, o, b_copy(r, 8, act_at(r, o), act_at(r, o), o, xdn)),
        ]

    def when(cond, fn):
        if cond is None:
            fn()
        else:
            pl.when(cond)(fn)

    def b_start(r):
        for cond, cp in b_own(r):
            when(cond, cp.start)

    def b_step1(r):
        remote(pact.at[r], pact.at[r], b_s.at[r, 0], b_r.at[r, 8], sib).wait_recv()
        for cond, cp in b_partner(r):
            when(cond, cp.start)

        @pl.when(zl == 1)
        def _():
            acts[r, :, pl.ds(pl.multiple_of(mp * FS, FS), FS)] = pact[r]

    def b_pass(r, relays):
        for cond, slot, cp in relays(r):

            def go(slot=slot, cp=cp):
                if isinstance(slot, int) and slot == 9:
                    remote(bact.at[r], bact.at[r], b_s.at[r, 0], b_r.at[r, 9], sib).wait_recv()
                else:
                    b_wait(r, slot)
                cp.start()

            when(cond, go)

    def b_finish(r):
        for cond, slots in ((x == 1, (0, 1)), (x == 2, (0, 1, 3)), (x == 3, (2, 3, 4, 5))):
            when(cond, lambda slots=slots: [b_wait(r, l) for l in slots] and None)

    def b_drain(r):
        for cond, cp in b_own(r) + b_partner(r):
            when(cond, cp.wait_send)
        for cond, _, cp in b_relay_a(r) + b_relay_b(r):
            when(cond, cp.wait_send)

    def clear():
        for l in range(1, LAYERS):

            @pl.when(l > m)
            def _(l=l):
                acts[:, :, l * FS : (l + 1) * FS] = jnp.zeros((CH, CR, FS), BF16)

    def norm_copy(k):
        return remote(nrecv.at[m], nrecv.at[m], n_s.at[0], n_r.at[0], ((m + k) % LAYERS, t))

    def norm_all():
        ref = nrecv.at[pl.ds(0, LAYERS - 1)]
        return remote(ref, ref, n_s.at[0], n_r.at[0], sib)

    def norms(lo, hi):
        for k in range(lo, hi):
            local[4 + k].wait()

        @pl.loop(lo, hi)
        def _(l):
            part = jnp.zeros((FS, 128), F32)
            for j in range(D // 128):
                v = w[pl.ds(pl.multiple_of(l * FS, FS), FS), j * 128 : (j + 1) * 128].astype(F32)
                part = part + v * v
            row = lax.dot_general(
                jnp.ones((8, 128), F32), part, NT_DIMS,
                preferred_element_type=F32, precision=lax.Precision.HIGHEST,
            )
            keep = jnp.where(l <= m, 1.0, 0.0).astype(F32)
            nrecv[m, pl.ds(l, 1), :] = row[0:1] * keep

        if hi == LAYERS:
            for k in range(1, LAYERS):
                norm_copy(k).start()

    def norms_finish():
        norm_all().wait_recv()
        total = nrecv[0]
        for s in range(1, LAYERS):
            total = total + nrecv[s]
        no_ref[...] = jnp.sqrt(total + 1e-06)

    def decode(r, h):
        rows = jnp.concatenate(
            [
                acts[r, pl.ds(pl.multiple_of((1 - c) * 128, 128), 128), :],
                acts[r, pl.ds(pl.multiple_of(c * 128, 128), 128), :],
            ],
            axis=0,
        )

        @pl.loop(h * HS, (h + 1) * HS)
        def _(n):
            part = jnp.dot(
                rows, w[:, pl.ds(pl.multiple_of(n * NT, NT), NT)], preferred_element_type=F32
            )
            part = part - jnp.dot(
                hit[r], tbuf[:, pl.ds(pl.multiple_of(n * NT, NT), NT)], preferred_element_type=F32
            )
            sibs[r, n] = part[:128].astype(BF16)
            opart[r, n] = part[128:]
            remote(sibs.at[r, n], sibr.at[r, n], cs_s.at[r], cs_r.at[r, h], sib).start()

    def cols(n):
        return slice(n * NT, (n + 1) * NT)

    def steps(h):
        return range(h * HS, (h + 1) * HS)

    def chip_sum(r, q, n):
        rows = pl.ds(pl.multiple_of(q * PR, PR), PR)
        return opart[r, n, rows, :] + sibr[r, n, rows, :].astype(F32)

    def c_copy(r, h, src, dst, dev):
        return remote(
            ys.at[r, src, :, half(h)], yr.at[r, dst, :, half(h)], cy_s.at[r, h], cy_r.at[r, h], dev
        )

    def c_all(r, h):
        ref = ys.at[r, pl.ds(0, 7), :, half(h)]
        return remote(ref, ref, cy_s.at[r, h], cy_r.at[r, h], sib)

    def c_a(r, h):
        ref = sibr.at[r, pl.ds(h * HS, HS)]
        remote(ref, ref, cs_s.at[r], cs_r.at[r, h], sib).wait_recv()
        for q, dev in peers:
            for n in steps(h):
                ys[r, q, :, cols(n)] = chip_sum(r, q, n).astype(BF16)
            c_copy(r, h, q, place, dev).start()

    def place_targets():
        tbuf[2 * PR :, :] = jnp.zeros((128 - 2 * PR, D), BF16)
        own_rows = (
            lax.broadcasted_iota(jnp.int32, (ROWS, 128), 0)
            == lax.broadcasted_iota(jnp.int32, (ROWS, 128), 1) + 2 * PR * t
        ) & (lax.broadcasted_iota(jnp.int32, (ROWS, 128), 1) < 2 * PR)
        own_rows = own_rows.astype(F32).astype(BF16)
        row = lax.broadcasted_iota(jnp.int32, (CR, ROWS), 0)
        core = (row // 128 + 1 - c) % 2
        base = 2 * PR * (2 * ((row % 128) // PR) + core) + row % PR
        wanted = jnp.broadcast_to(order_ref[...], (CR, ROWS))
        for r in range(CH):
            found = (wanted == base + PR * r).astype(F32).astype(BF16)
            hit[r] = jnp.dot(found, own_rows, preferred_element_type=F32).astype(BF16)

    def c_d(r, h):
        c_all(r, h).wait_recv()
        for n in steps(h):
            total = chip_sum(r, place, n)
            for q, _ in peers:
                total = total + yr[r, q, :, cols(n)].astype(F32)
            resid = (total + db_ref[:, cols(n)]) * SCALE
            rbuf[r, own_core, :, cols(n)] = resid.astype(BF16)
        ar[r][h].start()

    def f_copy(r, k, src, slot, dev):
        return remote(src, frecv.at[r, slot], f_s.at[r, k], f_r.at[r, slot], dev)

    def f_wait(r, slot):
        remote(frecv.at[r, slot], frecv.at[r, slot], f_s.at[r, 0], f_r.at[r, slot], sib).wait_recv()

    def f_sends(r, name):
        return {
            "a1": lambda: [f_copy(r, 0, gb.at[r, 0], 0, xdn)],
            "s1": lambda: [f_copy(r, 1, gb.at[r, 1], 1, xdn)],
            "a2": lambda: [
                f_copy(r, 0, gb.at[r, 0], 2, xup),
                f_copy(r, 1, gb.at[r, 1], 4, xdn),
            ],
            "a3": lambda: [f_copy(r, 3, gb.at[r, 3], 4, xup), f_copy(r, 2, gb.at[r, 2], 4, xdn)],
            "b2": lambda: [f_copy(r, 3, gb.at[r, 3], 1, xdn)],
            "s2": lambda: [f_copy(r, 2, gb.at[r, 2], 0, xdn)],
            "b3": lambda: [f_copy(r, 4 + l, gb.at[r, 4 + l], l, xdn) for l in (0, 1)],
            "c3": lambda: [f_copy(r, 1, gb.at[r, 1], 3, xup)],
            "s3": lambda: [f_copy(r, 0, gb.at[r, 0], 2, xup)],
            "r0": lambda: [f_copy(r, 7, frecv.at[r, 4], 2, xup)],
        }[name]()

    def f_go(r, name, before=None):
        @pl.when(x == int(name[1]))
        def _():
            if before is not None:
                before()
            for cp in f_sends(r, name):
                cp.start()

    def grads(r, i):
        @pl.when(i <= x)
        def _():
            p = (i + x // 3) % 3 if i < 3 else 3
            g = lax.dot_general(
                rbuf[r].reshape(CR, D), w[pl.ds(pl.multiple_of(p * 2 * FS, 2 * FS), 2 * FS), :],
                NT_DIMS, preferred_element_type=F32,
            )

            @pl.when(x != i)
            def _():
                gb[r, 2 * p] = g[:, :FS].astype(BF16)
                gb[r, 2 * p + 1] = g[:, FS:].astype(BF16)

            @pl.when(x == i)
            def _():
                gown[r, 0] = g[:, :FS]
                gown[r, 1] = g[:, FS:] * zl.astype(F32)

        def add(pairs):
            def fn():
                for l, slot in pairs:
                    f_wait(r, slot)
                    gb[r, l] = (gb[r, l].astype(F32) + frecv[r, slot].astype(F32)).astype(BF16)

            return fn

        if i == 0:
            for name in ("a1", "a2", "a3"):
                f_go(r, name)
        if i == 1:
            f_go(r, "b2")
            f_go(r, "b3")
        if i == 2:
            f_go(r, "c3")

    def f_add(r):
        def add(l, slot):
            def fn():
                f_wait(r, slot)
                gb[r, l] = (gb[r, l].astype(F32) + frecv[r, slot].astype(F32)).astype(BF16)

            return fn

        f_go(r, "s1", add(1, 4))
        f_go(r, "s2", add(2, 4))
        f_go(r, "s3", add(0, 2))

    def f_relay(r):
        f_go(r, "r0", lambda: f_wait(r, 4))

    def f_zcopy(r):
        return remote(fzs.at[r], fzr.at[r], fz_s.at[r], fz_r.at[r], zpl)

    def f_fin1(r):
        for cond, adds in (
            (x == 0, ((0, 0), (1, 1), (0, 2), (1, 3))),
            (x == 1, ((0, 0), (1, 1), (1, 2))),
            (x == 2, ((0, 0), (1, 1))),
        ):

            @pl.when(cond)
            def _(adds=adds):
                for j, slot in adds:
                    f_wait(r, slot)
                    gown[r, j] = gown[r, j] + frecv[r, slot].astype(F32)

        fzs[r] = gown[r, 1 - zl].astype(BF16)
        f_zcopy(r).start()

    def f_fin2(r):
        remote(fzr.at[r], fzr.at[r], fz_s.at[r], fz_r.at[r], sib).wait_recv()
        total = gown[r, zl] + fzr[r].astype(F32)
        norm = no_ref[pl.ds(m, 1), :]
        grad = jnp.where(pre[r] > 0, total + norm * SCALE, 0.0)
        go[r] = grad.astype(BF16)
        fsum = jnp.sum(grad, axis=0, keepdims=True)
        fo[...] = fsum if r == 0 else fo[...] + fsum

    def flip(r):
        @pl.loop(0, LAYERS)
        def _(l):
            block = acts[r, :, pl.ds(pl.multiple_of(l * FS, FS), FS)]
            act_t[l, :, r * CR : (r + 1) * CR] = block.T

    def dec_zero():
        for l in range(1, LAYERS):

            @pl.when(l > m)
            def _(l=l):
                do[l] = jnp.zeros((FS, D), BF16)

    def dec_grads(lo, hi):
        @pl.loop(lo, hi)
        def _(l):
            @pl.when(l <= m)
            def _():
                a_t = act_t[l]
                sums = jnp.dot(a_t, jnp.ones((ROWS, 128), BF16), preferred_element_type=F32)
                pick = (lax.broadcasted_iota(jnp.int32, (LAYERS, 128), 0) == l).astype(F32)
                norm = lax.dot_general(
                    no_ref[...], pick, TN_DIMS,
                    preferred_element_type=F32, precision=lax.Precision.HIGHEST,
                )
                factor = jnp.concatenate([sums * SCALE / norm] * 4, axis=1)
                rows = pl.ds(pl.multiple_of(l * FS, FS), FS)
                for n in range(NSTEPS):
                    part = jnp.dot(
                        a_t, rbuf[:, :, :, cols(n)].reshape(ROWS, NT), preferred_element_type=F32
                    )
                    do[l, :, cols(n)] = (part + factor * w[rows, cols(n)].astype(F32)).astype(BF16)

    def out_sum():
        ones = jnp.ones((8, ROWS), BF16)
        oo[...] = jnp.dot(ones, rbuf[...].reshape(ROWS, D), preferred_element_type=F32)[0:1]

    for k in range(2):
        local[k].wait()
    ax[0].start()
    clear()
    dec_zero()
    norms(0, 4)
    place_targets()
    ax[0].sent()
    ax[1].start()
    local[2].wait()
    local[3].wait()
    ax[0].take()
    ax[0].finish()
    encode(0)
    b_start(0)
    ax[1].take()
    b_step1(0)
    b_pass(0, b_relay_a)
    ax[1].finish()
    encode(1)
    b_start(1)
    norms(4, 8)
    b_pass(0, b_relay_b)
    b_step1(1)
    b_pass(1, b_relay_a)
    b_finish(0)
    decode(0, 0)
    c_a(0, 0)
    decode(0, 1)
    c_a(0, 1)
    b_pass(1, b_relay_b)
    c_d(0, 0)
    b_finish(1)
    c_d(0, 1)
    decode(1, 0)
    c_a(1, 0)
    decode(1, 1)
    c_a(1, 1)
    ar[0][0].take()
    ar[0][1].take()
    c_d(1, 0)
    c_d(1, 1)
    ar[0][0].finish()
    ar[0][1].finish()
    grads(0, 0)
    grads(0, 1)
    grads(0, 2)
    grads(0, 3)
    ar[1][0].take()
    ar[1][1].take()
    f_add(0)
    flip(0)
    norms_finish()
    ar[1][0].finish()
    ar[1][1].finish()
    grads(1, 0)
    grads(1, 1)
    grads(1, 2)
    f_relay(0)
    grads(1, 3)
    f_fin1(0)
    flip(1)
    out_sum()
    dec_grads(0, 1)
    f_add(1)
    dec_grads(1, 2)
    f_relay(1)
    f_fin2(0)
    f_fin1(1)
    dec_grads(2, 8)
    f_fin2(1)

    for g in ax + ar[0] + ar[1]:
        if g is not ax[0]:
            g.sent()
        g.drain()
    for r in range(CH):
        b_drain(r)
        remote(sibs.at[r], sibr.at[r], cs_s.at[r], cs_r.at[r, 0], sib).wait_send()
        for h in range(HALVES):
            c_all(r, h).wait_send()
        for name in ("a1", "s1", "a2", "a3", "b2", "s2", "b3", "c3", "s3", "r0"):

            @pl.when(x == int(name[1]))
            def _(name=name):
                for cp in f_sends(r, name):
                    cp.wait_send()

        f_zcopy(r).wait_send()
    norm_all().wait_send()


def run_main(x, tgt, order, we, eb, w, db):
    any_spec = pl.BlockSpec(memory_space=pl.ANY)
    vmem = pl.BlockSpec(memory_space=pltpu.VMEM)
    dma = pltpu.SemaphoreType.DMA
    return pl.pallas_call(
        main_kernel,
        out_shape=(
            pltpu.VMEM((CH, TOKS, PR, D), BF16),
            pltpu.VMEM((CH, CR, FS), BF16),
            pltpu.VMEM((LAYERS, FS, D), BF16),
            pltpu.VMEM((1, FS), F32),
            pltpu.VMEM((1, D), F32),
        ),
        in_specs=[any_spec, any_spec, vmem, any_spec, vmem, any_spec, vmem],
        out_specs=(vmem,) * 5,
        scratch_shapes=[
            pltpu.VMEM((128, D), BF16),
            pltpu.VMEM((CH, TOKS, PR, D), BF16),
            pltpu.VMEM((CH, CR, D), BF16),
            pltpu.VMEM((CH, CR, FS), BF16),
            pltpu.VMEM((CH, CR, FS), BF16),
            pltpu.VMEM((CH, CR, FS), F32),
            pltpu.VMEM((D, FS), BF16),
            pltpu.VMEM((LAYERS * FS, D), BF16),
            pltpu.VMEM((CH, NSTEPS, 128, NT), F32),
            pltpu.VMEM((CH, NSTEPS, 128, NT), BF16),
            pltpu.VMEM((CH, NSTEPS, 128, NT), BF16),
            pltpu.VMEM((CH, 8, PR, D), BF16),
            pltpu.VMEM((CH, 8, PR, D), BF16),
            pltpu.VMEM((CH, CR, 128), BF16),
            pltpu.VMEM((CH, LAYERS, CR, FS), BF16),
            pltpu.VMEM((CH, 2, CR, FS), F32),
            pltpu.VMEM((CH, 5, CR, FS), BF16),
            pltpu.VMEM((CH, CR, FS), BF16),
            pltpu.VMEM((CH, CR, FS), BF16),
            pltpu.VMEM((LAYERS, LAYERS, FS), F32),
            pltpu.VMEM((LAYERS, FS), F32),
            pltpu.VMEM((LAYERS, FS, ROWS), BF16),
            dma((4 + LAYERS,)), dma((CH + CH * HALVES, 2)), dma((CH + CH * HALVES, 2)),
            dma((CH, 9)), dma((CH, 10)), dma((CH,)), dma((CH, HALVES)),
            dma((CH, HALVES)), dma((CH, HALVES)),
            dma((CH, 8)), dma((CH, 5)), dma((CH,)), dma((CH,)),
            dma((1,)), dma((1,)),
        ],
        compiler_params=pltpu.CompilerParams(
            collective_id=0, has_side_effects=True, vmem_limit_bytes=46 << 20
        ),
        name="window",
    )(x, tgt, order, we, eb, w, db)


def tail_kernel(x_ref, g_ref, d_ref, f_ref, o_ref, dw_hbm, dwe_hbm, fg_hbm, og_hbm, enc, sems):
    copies = [
        pltpu.make_async_copy(d_ref.at[l], dw_hbm.at[0, l], sems.at[l]) for l in range(LAYERS)
    ]
    copies += [
        pltpu.make_async_copy(f_ref, fg_hbm, sems.at[LAYERS]),
        pltpu.make_async_copy(o_ref, og_hbm, sems.at[LAYERS + 1]),
    ]
    for cp in copies:
        cp.start()
    g = g_ref[...].reshape(ROWS, FS).T
    for n in range(NSTEPS):
        cs = slice(n * NT, (n + 1) * NT)
        part = jnp.dot(g, x_ref[:, :, :, cs].reshape(ROWS, NT), preferred_element_type=F32)
        enc[cs, :] = part.astype(BF16).T
    copies.append(pltpu.make_async_copy(enc, dwe_hbm.at[0], sems.at[LAYERS + 2]))
    copies[-1].start()
    for cp in copies:
        cp.wait()


def run_tail(xs, gl, dec, fg, og):
    any_spec = pl.BlockSpec(memory_space=pl.ANY)
    vmem = pl.BlockSpec(memory_space=pltpu.VMEM)
    return pl.pallas_call(
        tail_kernel,
        out_shape=(
            jax.ShapeDtypeStruct((1, LAYERS, FS, D), BF16),
            jax.ShapeDtypeStruct((1, D, FS), BF16),
            jax.ShapeDtypeStruct((1, FS), F32),
            jax.ShapeDtypeStruct((1, D), F32),
        ),
        in_specs=[vmem] * 5,
        out_specs=(any_spec,) * 4,
        scratch_shapes=[pltpu.VMEM((D, FS), BF16), pltpu.SemaphoreType.DMA((LAYERS + 3,))],
        compiler_params=pltpu.CompilerParams(vmem_limit_bytes=20 << 20),
        name="weights",
    )(xs, gl, dec, fg, og)


def on_device(x, tgt, order, we, eb, w, db):
    xs, gl, dec, fg, og = run_main(x, tgt, order[None], we, eb, w, db)
    dw, dwe, fg, og = run_tail(xs, gl, dec, fg, og)
    return dwe, fg, dw, og


def solution(mesh):
    placed = (
        P("layer", "tok", None),
        P("layer", "tok", None),
        P(),
        P("layer", None, "tok"),
        P("layer", "tok"),
        P("layer", None, "tok", None),
        P("layer", None),
    )
    return jax.shard_map(
        on_device,
        mesh=mesh,
        in_specs=placed,
        out_specs=(
            P("layer", None, "tok"),
            P("layer", "tok"),
            P("layer", None, "tok", None),
            P("layer", None),
        ),
        check_vma=False,
    )
```

```python
import math

import jax
import jax.numpy as jnp
from jax import lax
from jax.experimental import pallas as pl
from jax.experimental.pallas import tpu as pltpu
from jax.sharding import PartitionSpec as P

MESH = pl.DeviceIdType.MESH
F32, BF16 = jnp.float32, jnp.bfloat16
NT_DIMS = (((1,), (1,)), ((), ()))
TN_DIMS = (((0,), (0,)), ((), ()))

LAYERS = 8
TOKS = 16
ROWS = 512
D = 2048
FS = 256
CH = 2
PR = 16
CR = TOKS * PR
NT = 512
NSTEPS = D // NT
HALVES = 2
HW = D // HALVES
HS = NSTEPS // HALVES
SCALE = 1.0 / math.sqrt(ROWS)


def main_kernel(
    x_hbm, t_hbm, order_ref, we_hbm, eb_ref, w_hbm, db_ref,
    xo, go, do, fo, oo,
    tbuf, rbuf, acts, pact, bact, pre, we, w,
    opart, sibs, sibr, ys, yr, hit,
    gb, gown, frecv, fzs, fzr, nrecv, no_ref, act_t,
    lsem, ag_s, ag_r, b_s, b_r, cs_s, cs_r, cy_s, cy_r,
    f_s, f_r, fz_s, fz_r, n_s, n_r,
):
    m, t = lax.axis_index("layer"), lax.axis_index("tok")
    x, zl = m // 2, m % 2
    y, zh, c = t // 4, (t // 2) % 2, t % 2
    xp, xm = (x + 1) % 4, (x + 3) % 4

    def tk(yy, zz, cc):
        return 4 * yy + 2 * zz + cc

    sib = (m, tk(y, zh, 1 - c))
    others = [
        ((y + dy) % 4, (zh + dz) % 2) for dy, dz in ((2, 1), (1, 1), (3, 1), (2, 0), (0, 1), (1, 0), (3, 0))
    ]
    peers = [(2 * yy + zz, (m, tk(yy, zz, c))) for yy, zz in others]
    place = 2 * y + zh
    xup, xdn = (2 * xp + zl, t), (2 * xm + zl, t)
    mp = m + 1 - 2 * zl
    zpl = (mp, t)

    def remote(src, dst, s, r, dev):
        return pltpu.make_async_remote_copy(
            src_ref=src, dst_ref=dst, send_sem=s, recv_sem=r, device_id=dev, device_id_type=MESH
        )

    local = []

    def fetch(src, dst, k):
        cp = pltpu.make_async_copy(src, dst, lsem.at[k])
        cp.start()
        local.append(cp)

    own_core = 8 * c + place
    for r in range(CH):
        fetch(x_hbm.at[0, pl.ds(r * PR, PR)], xo.at[r, own_core], r)
    fetch(we_hbm.at[0], we, 2)
    fetch(t_hbm.at[0], tbuf.at[pl.ds(0, 2 * PR)], 3)
    for l in range(LAYERS):
        fetch(w_hbm.at[0, l], w.at[pl.ds(l * FS, FS)], 4 + l)

    barrier = pltpu.get_barrier_semaphore()
    for dev in [sib] + [dev for _, dev in peers]:
        pl.semaphore_signal(barrier, inc=1, device_id=dev, device_id_type=MESH)
    for k in range(1, LAYERS):
        pl.semaphore_signal(barrier, inc=1, device_id=((m + k) % LAYERS, t), device_id_type=MESH)
    pl.semaphore_wait(barrier, 8 + LAYERS - 1)

    class Gather:
        def __init__(self, inst, at):
            self.inst, self.at = inst, at

        def copy(self, core, first, number, k, dev):
            ref = self.at(core, first, number)
            return remote(ref, ref, ag_s.at[self.inst, k], ag_r.at[self.inst, k], dev)

        def start(self):
            for _, dev in peers:
                self.copy(c, place, 1, 0, dev).start()

        def sent(self):
            self.copy(c, 0, 7, 0, sib).wait_send()

        def take(self):
            self.copy(c, 0, 7, 0, sib).wait_recv()
            self.copy(c, 0, 8, 1, sib).start()

        def finish(self):
            self.copy(1 - c, 0, 8, 1, sib).wait_recv()

        def drain(self):
            self.copy(c, 0, 8, 1, sib).wait_send()

    def half(h):
        return slice(h * HW, (h + 1) * HW)

    ax = [Gather(r, lambda cc, f, n, r=r: xo.at[r, pl.ds(8 * cc + f, n)]) for r in range(CH)]
    ar = [
        [
            Gather(
                CH + HALVES * r + h,
                lambda cc, f, n, r=r, h=h: rbuf.at[r, pl.ds(8 * cc + f, n), :, half(h)],
            )
            for h in range(HALVES)
        ]
        for r in range(CH)
    ]

    def encode(r):
        rows = xo[r].reshape(CR, D)
        value = jnp.dot(rows, we[...], preferred_element_type=F32) + eb_ref[...]
        pre[r] = value
        acts[r, :, pl.ds(pl.multiple_of(m * FS, FS), FS)] = jnp.maximum(value, 0.0).astype(BF16)

    def act_at(r, l):
        return acts.at[r, :, pl.ds(pl.multiple_of(l * FS, FS), FS)]

    def b_copy(r, k, src, dst, slot, dev):
        return remote(src, dst, b_s.at[r, k], b_r.at[r, slot], dev)

    def b_wait(r, l):
        b_copy(r, 0, act_at(r, l), act_at(r, l), l, sib).wait_recv()

    def b_own(r):
        return [
            (None, b_copy(r, 0, act_at(r, m), pact.at[r], 8, zpl)),
            (x < 3, b_copy(r, 1, act_at(r, m), act_at(r, m), m, xup)),
            (x == 0, b_copy(r, 2, act_at(r, m), act_at(r, m), m, xdn)),
            (m == 3, b_copy(r, 3, act_at(r, m), bact.at[r], 9, xdn)),
        ]

    def b_partner(r):
        return [
            (x < 3, b_copy(r, 4, pact.at[r], act_at(r, mp), mp, xup)),
            (x == 0, b_copy(r, 5, pact.at[r], act_at(r, mp), mp, xdn)),
            (m == 2, b_copy(r, 6, pact.at[r], bact.at[r], 9, xdn)),
        ]

    def b_relay_a(r):
        return [
            (m == 1, 9, b_copy(r, 7, bact.at[r], act_at(r, 3), 3, xdn)),
            (m == 4, 2, b_copy(r, 7, act_at(r, 2), act_at(r, 2), 2, xup)),
            (x == 3, zl, b_copy(r, 7, act_at(r, zl), act_at(r, zl), zl, xdn)),
        ]

    def b_relay_b(r):
        o = 1 - zl
        return [
            (m == 0, 9, b_copy(r, 7, bact.at[r], act_at(r, 3), 3, xdn)),
            (m == 5, 2, b_copy(r, 7, act_at(r, 2), act_at(r, 2), 2, xup)),
            (x == 3, o, b_copy(r, 8, act_at(r, o), act_at(r, o), o, xdn)),
        ]

    def when(cond, fn):
        if cond is None:
            fn()
        else:
            pl.when(cond)(fn)

    def b_start(r):
        for cond, cp in b_own(r):
            when(cond, cp.start)

    def b_step1(r):
        remote(pact.at[r], pact.at[r], b_s.at[r, 0], b_r.at[r, 8], sib).wait_recv()
        for cond, cp in b_partner(r):
            when(cond, cp.start)

        @pl.when(zl == 1)
        def _():
            acts[r, :, pl.ds(pl.multiple_of(mp * FS, FS), FS)] = pact[r]

    def b_pass(r, relays):
        for cond, slot, cp in relays(r):

            def go(slot=slot, cp=cp):
                if isinstance(slot, int) and slot == 9:
                    remote(bact.at[r], bact.at[r], b_s.at[r, 0], b_r.at[r, 9], sib).wait_recv()
                else:
                    b_wait(r, slot)
                cp.start()

            when(cond, go)

    def b_finish(r):
        for cond, slots in ((x == 1, (0, 1)), (x == 2, (0, 1, 3)), (x == 3, (2, 3, 4, 5))):
            when(cond, lambda slots=slots: [b_wait(r, l) for l in slots] and None)

    def b_drain(r):
        for cond, cp in b_own(r) + b_partner(r):
            when(cond, cp.wait_send)
        for cond, _, cp in b_relay_a(r) + b_relay_b(r):
            when(cond, cp.wait_send)

    def clear():
        for l in range(1, LAYERS):

            @pl.when(l > m)
            def _(l=l):
                acts[:, :, l * FS : (l + 1) * FS] = jnp.zeros((CH, CR, FS), BF16)

    def norm_copy(k):
        return remote(nrecv.at[m], nrecv.at[m], n_s.at[0], n_r.at[0], ((m + k) % LAYERS, t))

    def norm_all():
        ref = nrecv.at[pl.ds(0, LAYERS - 1)]
        return remote(ref, ref, n_s.at[0], n_r.at[0], sib)

    def norms(lo, hi):
        for k in range(lo, hi):
            local[4 + k].wait()

        @pl.loop(lo, hi)
        def _(l):
            part = jnp.zeros((FS, 128), F32)
            for j in range(D // 128):
                v = w[pl.ds(pl.multiple_of(l * FS, FS), FS), j * 128 : (j + 1) * 128].astype(F32)
                part = part + v * v
            row = lax.dot_general(
                jnp.ones((8, 128), F32), part, NT_DIMS,
                preferred_element_type=F32, precision=lax.Precision.HIGHEST,
            )
            keep = jnp.where(l <= m, 1.0, 0.0).astype(F32)
            nrecv[m, pl.ds(l, 1), :] = row[0:1] * keep

        if hi == LAYERS:
            for k in range(1, LAYERS):
                norm_copy(k).start()

    def norms_finish():
        norm_all().wait_recv()
        total = nrecv[0]
        for s in range(1, LAYERS):
            total = total + nrecv[s]
        no_ref[...] = jnp.sqrt(total + 1e-06)

    def decode(r, h):
        rows = jnp.concatenate(
            [
                acts[r, pl.ds(pl.multiple_of((1 - c) * 128, 128), 128), :],
                acts[r, pl.ds(pl.multiple_of(c * 128, 128), 128), :],
            ],
            axis=0,
        )

        @pl.loop(h * HS, (h + 1) * HS)
        def _(n):
            part = jnp.dot(
                rows, w[:, pl.ds(pl.multiple_of(n * NT, NT), NT)], preferred_element_type=F32
            )
            part = part - jnp.dot(
                hit[r], tbuf[:, pl.ds(pl.multiple_of(n * NT, NT), NT)], preferred_element_type=F32
            )
            sibs[r, n] = part[:128].astype(BF16)
            opart[r, n] = part[128:]
            remote(sibs.at[r, n], sibr.at[r, n], cs_s.at[r], cs_r.at[r, h], sib).start()

    def cols(n):
        return slice(n * NT, (n + 1) * NT)

    def steps(h):
        return range(h * HS, (h + 1) * HS)

    def chip_sum(r, q, n):
        rows = pl.ds(pl.multiple_of(q * PR, PR), PR)
        return opart[r, n, rows, :] + sibr[r, n, rows, :].astype(F32)

    def c_copy(r, h, src, dst, dev):
        return remote(
            ys.at[r, src, :, half(h)], yr.at[r, dst, :, half(h)], cy_s.at[r, h], cy_r.at[r, h], dev
        )

    def c_all(r, h):
        ref = ys.at[r, pl.ds(0, 7), :, half(h)]
        return remote(ref, ref, cy_s.at[r, h], cy_r.at[r, h], sib)

    def c_a(r, h):
        ref = sibr.at[r, pl.ds(h * HS, HS)]
        remote(ref, ref, cs_s.at[r], cs_r.at[r, h], sib).wait_recv()
        for q, dev in peers:
            for n in steps(h):
                ys[r, q, :, cols(n)] = chip_sum(r, q, n).astype(BF16)
            c_copy(r, h, q, place, dev).start()

    def place_targets():
        tbuf[2 * PR :, :] = jnp.zeros((128 - 2 * PR, D), BF16)
        own_rows = (
            lax.broadcasted_iota(jnp.int32, (ROWS, 128), 0)
            == lax.broadcasted_iota(jnp.int32, (ROWS, 128), 1) + 2 * PR * t
        ) & (lax.broadcasted_iota(jnp.int32, (ROWS, 128), 1) < 2 * PR)
        own_rows = own_rows.astype(F32).astype(BF16)
        row = lax.broadcasted_iota(jnp.int32, (CR, ROWS), 0)
        core = (row // 128 + 1 - c) % 2
        base = 2 * PR * (2 * ((row % 128) // PR) + core) + row % PR
        wanted = jnp.broadcast_to(order_ref[...], (CR, ROWS))
        for r in range(CH):
            found = (wanted == base + PR * r).astype(F32).astype(BF16)
            hit[r] = jnp.dot(found, own_rows, preferred_element_type=F32).astype(BF16)

    def c_d(r, h):
        c_all(r, h).wait_recv()
        for n in steps(h):
            total = chip_sum(r, place, n)
            for q, _ in peers:
                total = total + yr[r, q, :, cols(n)].astype(F32)
            resid = (total + db_ref[:, cols(n)]) * SCALE
            rbuf[r, own_core, :, cols(n)] = resid.astype(BF16)
        ar[r][h].start()

    def f_copy(r, k, src, slot, dev):
        return remote(src, frecv.at[r, slot], f_s.at[r, k], f_r.at[r, slot], dev)

    def f_wait(r, slot):
        remote(frecv.at[r, slot], frecv.at[r, slot], f_s.at[r, 0], f_r.at[r, slot], sib).wait_recv()

    def f_sends(r, name):
        def to_owner(l, base):
            return f_copy(r, l, gb.at[r, l], base + zl, (l, t))

        return {
            "a1": lambda: [to_owner(0, 0)],
            "s1": lambda: [to_owner(1, 0)],
            "a2": lambda: [
                f_copy(r, 0, gb.at[r, 0], 2, xup),
                f_copy(r, 1, gb.at[r, 1], 4, xdn),
            ],
            "a3": lambda: [f_copy(r, 3, gb.at[r, 3], 4, xup), f_copy(r, 2, gb.at[r, 2], 4, xdn)],
            "b2": lambda: [to_owner(3, 0)],
            "s2": lambda: [to_owner(2, 0)],
            "b3": lambda: [to_owner(4, 0), to_owner(5, 0)],
            "c3": lambda: [to_owner(1, 2)],
            "s3": lambda: [to_owner(0, 2)],
            "r0": lambda: [f_copy(r, 7, frecv.at[r, 4], 2 + zl, (3, t))],
        }[name]()

    def f_go(r, name, before=None):
        @pl.when(x == int(name[1]))
        def _():
            if before is not None:
                before()
            for cp in f_sends(r, name):
                cp.start()

    def grads(r, i):
        @pl.when(i <= x)
        def _():
            p = (i + x // 3) % 3 if i < 3 else 3
            g = lax.dot_general(
                rbuf[r].reshape(CR, D), w[pl.ds(pl.multiple_of(p * 2 * FS, 2 * FS), 2 * FS), :],
                NT_DIMS, preferred_element_type=F32,
            )

            @pl.when(x != i)
            def _():
                gb[r, 2 * p] = g[:, :FS].astype(BF16)
                gb[r, 2 * p + 1] = g[:, FS:].astype(BF16)

            @pl.when(x == i)
            def _():
                gown[r, 0] = g[:, :FS]
                gown[r, 1] = g[:, FS:] * zl.astype(F32)

        def add(pairs):
            def fn():
                for l, slot in pairs:
                    f_wait(r, slot)
                    gb[r, l] = (gb[r, l].astype(F32) + frecv[r, slot].astype(F32)).astype(BF16)

            return fn

        if i == 0:
            for name in ("a1", "a2", "a3"):
                f_go(r, name)
        if i == 1:
            f_go(r, "b2")
            f_go(r, "b3")
        if i == 2:
            f_go(r, "c3")

    def f_add(r):
        def add(l, slot):
            def fn():
                f_wait(r, slot)
                gb[r, l] = (gb[r, l].astype(F32) + frecv[r, slot].astype(F32)).astype(BF16)

            return fn

        f_go(r, "s1", add(1, 4))
        f_go(r, "s2", add(2, 4))
        f_go(r, "s3", add(0, 2))

    def f_relay(r):
        f_go(r, "r0", lambda: f_wait(r, 4))

    def f_zcopy(r):
        return remote(fzs.at[r], fzr.at[r], fz_s.at[r], fz_r.at[r], zpl)

    def f_own(r):
        @pl.when(zl == 1)
        def _():
            fzs[r] = gown[r, 0].astype(BF16)
            f_zcopy(r).start()

    def f_fin(r):
        gown[r, 0] = jnp.where(zl == 1, gown[r, 1], gown[r, 0])

        @pl.when(zl == 0)
        def _():
            f_zcopy(r).wait_recv()
            gown[r, 0] = gown[r, 0] + fzr[r].astype(F32)

        for cond, slots in ((x < 3, (0, 1)), ((x == 0) | (m == 3), (2, 3))):

            @pl.when(cond)
            def _(slots=slots):
                for slot in slots:
                    f_wait(r, slot)
                    gown[r, 0] = gown[r, 0] + frecv[r, slot].astype(F32)

        norm = no_ref[pl.ds(m, 1), :]
        grad = jnp.where(pre[r] > 0, gown[r, 0] + norm * SCALE, 0.0)
        go[r] = grad.astype(BF16)
        fsum = jnp.sum(grad, axis=0, keepdims=True)
        fo[...] = fsum if r == 0 else fo[...] + fsum

    def flip(r):
        @pl.loop(0, LAYERS)
        def _(l):
            block = acts[r, :, pl.ds(pl.multiple_of(l * FS, FS), FS)]
            act_t[l, :, r * CR : (r + 1) * CR] = block.T

    def dec_zero():
        for l in range(1, LAYERS):

            @pl.when(l > m)
            def _(l=l):
                do[l] = jnp.zeros((FS, D), BF16)

    def dec_grads(lo, hi):
        @pl.loop(lo, hi)
        def _(l):
            @pl.when(l <= m)
            def _():
                a_t = act_t[l]
                sums = jnp.dot(a_t, jnp.ones((ROWS, 128), BF16), preferred_element_type=F32)
                pick = (lax.broadcasted_iota(jnp.int32, (LAYERS, 128), 0) == l).astype(F32)
                norm = lax.dot_general(
                    no_ref[...], pick, TN_DIMS,
                    preferred_element_type=F32, precision=lax.Precision.HIGHEST,
                )
                factor = jnp.concatenate([sums * SCALE / norm] * 4, axis=1)
                rows = pl.ds(pl.multiple_of(l * FS, FS), FS)
                for n in range(NSTEPS):
                    part = jnp.dot(
                        a_t, rbuf[:, :, :, cols(n)].reshape(ROWS, NT), preferred_element_type=F32
                    )
                    do[l, :, cols(n)] = (part + factor * w[rows, cols(n)].astype(F32)).astype(BF16)

    def out_sum():
        ones = jnp.ones((8, ROWS), BF16)
        oo[...] = jnp.dot(ones, rbuf[...].reshape(ROWS, D), preferred_element_type=F32)[0:1]

    for k in range(2):
        local[k].wait()
    ax[0].start()
    clear()
    dec_zero()
    norms(0, 4)
    place_targets()
    ax[0].sent()
    ax[1].start()
    local[2].wait()
    local[3].wait()
    ax[0].take()
    ax[0].finish()
    encode(0)
    b_start(0)
    ax[1].take()
    b_step1(0)
    b_pass(0, b_relay_a)
    ax[1].finish()
    encode(1)
    b_start(1)
    norms(4, 8)
    b_pass(0, b_relay_b)
    b_step1(1)
    b_pass(1, b_relay_a)
    b_finish(0)
    decode(0, 0)
    c_a(0, 0)
    decode(0, 1)
    c_a(0, 1)
    b_pass(1, b_relay_b)
    c_d(0, 0)
    b_finish(1)
    c_d(0, 1)
    decode(1, 0)
    c_a(1, 0)
    decode(1, 1)
    c_a(1, 1)
    ar[0][0].take()
    ar[0][1].take()
    c_d(1, 0)
    c_d(1, 1)
    ar[0][0].finish()
    ar[0][1].finish()
    grads(0, 0)
    grads(0, 1)
    grads(0, 2)
    grads(0, 3)
    f_own(0)
    ar[1][0].take()
    ar[1][1].take()
    f_add(0)
    flip(0)
    norms_finish()
    ar[1][0].finish()
    ar[1][1].finish()
    grads(1, 0)
    grads(1, 1)
    grads(1, 2)
    f_relay(0)
    grads(1, 3)
    f_own(1)
    flip(1)
    out_sum()
    dec_grads(0, 1)
    f_add(1)
    dec_grads(1, 2)
    f_relay(1)
    f_fin(0)
    dec_grads(2, 8)
    f_fin(1)

    for g in ax + ar[0] + ar[1]:
        if g is not ax[0]:
            g.sent()
        g.drain()
    for r in range(CH):
        b_drain(r)
        remote(sibs.at[r], sibr.at[r], cs_s.at[r], cs_r.at[r, 0], sib).wait_send()
        for h in range(HALVES):
            c_all(r, h).wait_send()
        for name in ("a1", "s1", "a2", "a3", "b2", "s2", "b3", "c3", "s3", "r0"):

            @pl.when(x == int(name[1]))
            def _(name=name):
                for cp in f_sends(r, name):
                    cp.wait_send()

        pl.when(zl == 1)(f_zcopy(r).wait_send)
    norm_all().wait_send()


def run_main(x, tgt, order, we, eb, w, db):
    any_spec = pl.BlockSpec(memory_space=pl.ANY)
    vmem = pl.BlockSpec(memory_space=pltpu.VMEM)
    dma = pltpu.SemaphoreType.DMA
    return pl.pallas_call(
        main_kernel,
        out_shape=(
            pltpu.VMEM((CH, TOKS, PR, D), BF16),
            pltpu.VMEM((CH, CR, FS), BF16),
            pltpu.VMEM((LAYERS, FS, D), BF16),
            pltpu.VMEM((1, FS), F32),
            pltpu.VMEM((1, D), F32),
        ),
        in_specs=[any_spec, any_spec, vmem, any_spec, vmem, any_spec, vmem],
        out_specs=(vmem,) * 5,
        scratch_shapes=[
            pltpu.VMEM((128, D), BF16),
            pltpu.VMEM((CH, TOKS, PR, D), BF16),
            pltpu.VMEM((CH, CR, D), BF16),
            pltpu.VMEM((CH, CR, FS), BF16),
            pltpu.VMEM((CH, CR, FS), BF16),
            pltpu.VMEM((CH, CR, FS), F32),
            pltpu.VMEM((D, FS), BF16),
            pltpu.VMEM((LAYERS * FS, D), BF16),
            pltpu.VMEM((CH, NSTEPS, 128, NT), F32),
            pltpu.VMEM((CH, NSTEPS, 128, NT), BF16),
            pltpu.VMEM((CH, NSTEPS, 128, NT), BF16),
            pltpu.VMEM((CH, 8, PR, D), BF16),
            pltpu.VMEM((CH, 8, PR, D), BF16),
            pltpu.VMEM((CH, CR, 128), BF16),
            pltpu.VMEM((CH, LAYERS, CR, FS), BF16),
            pltpu.VMEM((CH, 2, CR, FS), F32),
            pltpu.VMEM((CH, 5, CR, FS), BF16),
            pltpu.VMEM((CH, CR, FS), BF16),
            pltpu.VMEM((CH, CR, FS), BF16),
            pltpu.VMEM((LAYERS, LAYERS, FS), F32),
            pltpu.VMEM((LAYERS, FS), F32),
            pltpu.VMEM((LAYERS, FS, ROWS), BF16),
            dma((4 + LAYERS,)), dma((CH + CH * HALVES, 2)), dma((CH + CH * HALVES, 2)),
            dma((CH, 9)), dma((CH, 10)), dma((CH,)), dma((CH, HALVES)),
            dma((CH, HALVES)), dma((CH, HALVES)),
            dma((CH, 8)), dma((CH, 5)), dma((CH,)), dma((CH,)),
            dma((1,)), dma((1,)),
        ],
        compiler_params=pltpu.CompilerParams(
            collective_id=0, has_side_effects=True, vmem_limit_bytes=46 << 20
        ),
        name="window",
    )(x, tgt, order, we, eb, w, db)


def tail_kernel(x_ref, g_ref, d_ref, f_ref, o_ref, dw_hbm, dwe_hbm, fg_hbm, og_hbm, enc, sems):
    copies = [
        pltpu.make_async_copy(d_ref.at[l], dw_hbm.at[0, l], sems.at[l]) for l in range(LAYERS)
    ]
    copies += [
        pltpu.make_async_copy(f_ref, fg_hbm, sems.at[LAYERS]),
        pltpu.make_async_copy(o_ref, og_hbm, sems.at[LAYERS + 1]),
    ]
    for cp in copies:
        cp.start()
    g = g_ref[...].reshape(ROWS, FS).T
    for n in range(NSTEPS):
        cs = slice(n * NT, (n + 1) * NT)
        part = jnp.dot(g, x_ref[:, :, :, cs].reshape(ROWS, NT), preferred_element_type=F32)
        enc[cs, :] = part.astype(BF16).T
    copies.append(pltpu.make_async_copy(enc, dwe_hbm.at[0], sems.at[LAYERS + 2]))
    copies[-1].start()
    for cp in copies:
        cp.wait()


def run_tail(xs, gl, dec, fg, og):
    any_spec = pl.BlockSpec(memory_space=pl.ANY)
    vmem = pl.BlockSpec(memory_space=pltpu.VMEM)
    return pl.pallas_call(
        tail_kernel,
        out_shape=(
            jax.ShapeDtypeStruct((1, LAYERS, FS, D), BF16),
            jax.ShapeDtypeStruct((1, D, FS), BF16),
            jax.ShapeDtypeStruct((1, FS), F32),
            jax.ShapeDtypeStruct((1, D), F32),
        ),
        in_specs=[vmem] * 5,
        out_specs=(any_spec,) * 4,
        scratch_shapes=[pltpu.VMEM((D, FS), BF16), pltpu.SemaphoreType.DMA((LAYERS + 3,))],
        compiler_params=pltpu.CompilerParams(vmem_limit_bytes=20 << 20),
        name="weights",
    )(xs, gl, dec, fg, og)


def on_device(x, tgt, order, we, eb, w, db):
    xs, gl, dec, fg, og = run_main(x, tgt, order[None], we, eb, w, db)
    dw, dwe, fg, og = run_tail(xs, gl, dec, fg, og)
    return dwe, fg, dw, og


def solution(mesh):
    placed = (
        P("layer", "tok", None),
        P("layer", "tok", None),
        P(),
        P("layer", None, "tok"),
        P("layer", "tok"),
        P("layer", None, "tok", None),
        P("layer", None),
    )
    return jax.shard_map(
        on_device,
        mesh=mesh,
        in_specs=placed,
        out_specs=(
            P("layer", None, "tok"),
            P("layer", "tok"),
            P("layer", None, "tok", None),
            P("layer", None),
        ),
        check_vma=False,
    )
```

```python
import math

import jax
import jax.numpy as jnp
from jax import lax
from jax.experimental import pallas as pl
from jax.experimental.pallas import tpu as pltpu
from jax.sharding import PartitionSpec as P

MESH = pl.DeviceIdType.MESH
F32, BF16 = jnp.float32, jnp.bfloat16
NT_DIMS = (((1,), (1,)), ((), ()))
TN_DIMS = (((0,), (0,)), ((), ()))

LAYERS = 8
TOKS = 16
ROWS = 512
D = 2048
FS = 256
CH = 2
PR = 16
CR = TOKS * PR
NT = 512
NSTEPS = D // NT
HALVES = 2
HW = D // HALVES
HS = NSTEPS // HALVES
SCALE = 1.0 / math.sqrt(ROWS)


def main_kernel(
    x_hbm, t_hbm, order_ref, we_hbm, eb_ref, w_hbm, db_ref,
    xo, go, do, fo, oo,
    tbuf, rbuf, acts, pact, bact, pre, we, w,
    opart, sibs, sibr, ys, yr, hit,
    gb, gown, frecv, fzs, fzr, nrecv, no_ref, act_t,
    lsem, ag_s, ag_r, b_s, b_r, cs_s, cs_r, cy_s, cy_r,
    f_s, f_r, fz_s, fz_r, n_s, n_r,
):
    m, t = lax.axis_index("layer"), lax.axis_index("tok")
    x, zl = m // 2, m % 2
    y, zh, c = t // 4, (t // 2) % 2, t % 2
    xp, xm = (x + 1) % 4, (x + 3) % 4

    def tk(yy, zz, cc):
        return 4 * yy + 2 * zz + cc

    sib = (m, tk(y, zh, 1 - c))
    others = [
        ((y + dy) % 4, (zh + dz) % 2) for dy, dz in ((2, 1), (1, 1), (3, 1), (2, 0), (0, 1), (1, 0), (3, 0))
    ]
    peers = [(2 * yy + zz, (m, tk(yy, zz, c))) for yy, zz in others]
    place = 2 * y + zh
    xup, xdn = (2 * xp + zl, t), (2 * xm + zl, t)
    mp = m + 1 - 2 * zl
    zpl = (mp, t)

    def remote(src, dst, s, r, dev):
        return pltpu.make_async_remote_copy(
            src_ref=src, dst_ref=dst, send_sem=s, recv_sem=r, device_id=dev, device_id_type=MESH
        )

    local = []

    def fetch(src, dst, k):
        cp = pltpu.make_async_copy(src, dst, lsem.at[k])
        cp.start()
        local.append(cp)

    own_core = 8 * c + place
    for r in range(CH):
        fetch(x_hbm.at[0, pl.ds(r * PR, PR)], xo.at[r, own_core], r)
    fetch(we_hbm.at[0], we, 2)
    fetch(t_hbm.at[0], tbuf.at[pl.ds(0, 2 * PR)], 3)
    for l in range(LAYERS):
        fetch(w_hbm.at[0, l], w.at[pl.ds(l * FS, FS)], 4 + l)

    barrier = pltpu.get_barrier_semaphore()
    for dev in [sib] + [dev for _, dev in peers]:
        pl.semaphore_signal(barrier, inc=1, device_id=dev, device_id_type=MESH)
    for k in range(1, LAYERS):
        pl.semaphore_signal(barrier, inc=1, device_id=((m + k) % LAYERS, t), device_id_type=MESH)
    pl.semaphore_wait(barrier, 8 + LAYERS - 1)

    class Gather:
        def __init__(self, inst, at):
            self.inst, self.at = inst, at

        def copy(self, core, first, number, k, dev):
            ref = self.at(core, first, number)
            return remote(ref, ref, ag_s.at[self.inst, k], ag_r.at[self.inst, k], dev)

        def start(self):
            for _, dev in peers:
                self.copy(c, place, 1, 0, dev).start()

        def sent(self):
            self.copy(c, 0, 7, 0, sib).wait_send()

        def take(self):
            self.copy(c, 0, 7, 0, sib).wait_recv()
            self.copy(c, 0, 8, 1, sib).start()

        def finish(self):
            self.copy(1 - c, 0, 8, 1, sib).wait_recv()

        def drain(self):
            self.copy(c, 0, 8, 1, sib).wait_send()

    def half(h):
        return slice(h * HW, (h + 1) * HW)

    ax = [Gather(r, lambda cc, f, n, r=r: xo.at[r, pl.ds(8 * cc + f, n)]) for r in range(CH)]
    ar = [
        [
            Gather(
                CH + HALVES * r + h,
                lambda cc, f, n, r=r, h=h: rbuf.at[r, pl.ds(8 * cc + f, n), :, half(h)],
            )
            for h in range(HALVES)
        ]
        for r in range(CH)
    ]

    def encode(r):
        rows = xo[r].reshape(CR, D)
        value = jnp.dot(rows, we[...], preferred_element_type=F32) + eb_ref[...]
        pre[r] = value
        acts[r, :, pl.ds(pl.multiple_of(m * FS, FS), FS)] = jnp.maximum(value, 0.0).astype(BF16)

    def act_at(r, l):
        return acts.at[r, :, pl.ds(pl.multiple_of(l * FS, FS), FS)]

    def b_copy(r, k, src, dst, slot, dev):
        return remote(src, dst, b_s.at[r, k], b_r.at[r, slot], dev)

    def b_wait(r, l):
        b_copy(r, 0, act_at(r, l), act_at(r, l), l, sib).wait_recv()

    def b_own(r):
        return [
            (None, b_copy(r, 0, act_at(r, m), pact.at[r], 8, zpl)),
            (x < 3, b_copy(r, 1, act_at(r, m), act_at(r, m), m, xup)),
            (x == 0, b_copy(r, 2, act_at(r, m), act_at(r, m), m, xdn)),
            (m == 3, b_copy(r, 3, act_at(r, m), bact.at[r], 9, xdn)),
        ]

    def b_partner(r):
        return [
            (x < 3, b_copy(r, 4, pact.at[r], act_at(r, mp), mp, xup)),
            (x == 0, b_copy(r, 5, pact.at[r], act_at(r, mp), mp, xdn)),
            (m == 2, b_copy(r, 6, pact.at[r], bact.at[r], 9, xdn)),
        ]

    def b_relay_a(r):
        return [
            (m == 1, 9, b_copy(r, 7, bact.at[r], act_at(r, 3), 3, xdn)),
            (m == 4, 2, b_copy(r, 7, act_at(r, 2), act_at(r, 2), 2, xup)),
            (x == 3, zl, b_copy(r, 7, act_at(r, zl), act_at(r, zl), zl, xdn)),
        ]

    def b_relay_b(r):
        o = 1 - zl
        return [
            (m == 0, 9, b_copy(r, 7, bact.at[r], act_at(r, 3), 3, xdn)),
            (m == 5, 2, b_copy(r, 7, act_at(r, 2), act_at(r, 2), 2, xup)),
            (x == 3, o, b_copy(r, 8, act_at(r, o), act_at(r, o), o, xdn)),
        ]

    def when(cond, fn):
        if cond is None:
            fn()
        else:
            pl.when(cond)(fn)

    def b_start(r):
        for cond, cp in b_own(r):
            when(cond, cp.start)

    def b_step1(r):
        remote(pact.at[r], pact.at[r], b_s.at[r, 0], b_r.at[r, 8], sib).wait_recv()
        for cond, cp in b_partner(r):
            when(cond, cp.start)

        @pl.when(zl == 1)
        def _():
            acts[r, :, pl.ds(pl.multiple_of(mp * FS, FS), FS)] = pact[r]

    def b_pass(r, relays):
        for cond, slot, cp in relays(r):

            def go(slot=slot, cp=cp):
                if isinstance(slot, int) and slot == 9:
                    remote(bact.at[r], bact.at[r], b_s.at[r, 0], b_r.at[r, 9], sib).wait_recv()
                else:
                    b_wait(r, slot)
                cp.start()

            when(cond, go)

    def b_finish(r):
        for cond, slots in ((x == 1, (0, 1)), (x == 2, (0, 1, 3)), (x == 3, (2, 3, 4, 5))):
            when(cond, lambda slots=slots: [b_wait(r, l) for l in slots] and None)

    def b_drain(r):
        for cond, cp in b_own(r) + b_partner(r):
            when(cond, cp.wait_send)
        for cond, _, cp in b_relay_a(r) + b_relay_b(r):
            when(cond, cp.wait_send)

    def clear():
        for l in range(1, LAYERS):

            @pl.when(l > m)
            def _(l=l):
                acts[:, :, l * FS : (l + 1) * FS] = jnp.zeros((CH, CR, FS), BF16)

    def norm_copy(k):
        return remote(nrecv.at[m], nrecv.at[m], n_s.at[0], n_r.at[0], ((m + k) % LAYERS, t))

    def norm_all():
        ref = nrecv.at[pl.ds(0, LAYERS - 1)]
        return remote(ref, ref, n_s.at[0], n_r.at[0], sib)

    def norms(lo, hi):
        for k in range(lo, hi):
            local[4 + k].wait()

        @pl.loop(lo, hi)
        def _(l):
            part = jnp.zeros((FS, 128), F32)
            for j in range(D // 128):
                v = w[pl.ds(pl.multiple_of(l * FS, FS), FS), j * 128 : (j + 1) * 128].astype(F32)
                part = part + v * v
            row = lax.dot_general(
                jnp.ones((8, 128), F32), part, NT_DIMS,
                preferred_element_type=F32, precision=lax.Precision.HIGHEST,
            )
            keep = jnp.where(l <= m, 1.0, 0.0).astype(F32)
            nrecv[m, pl.ds(l, 1), :] = row[0:1] * keep

        if hi == LAYERS:
            for k in range(1, LAYERS):
                norm_copy(k).start()

    def norms_finish():
        norm_all().wait_recv()
        total = nrecv[0]
        for s in range(1, LAYERS):
            total = total + nrecv[s]
        no_ref[...] = jnp.sqrt(total + 1e-06)

    def decode(r, h):
        rows = jnp.concatenate(
            [
                acts[r, pl.ds(pl.multiple_of((1 - c) * 128, 128), 128), :],
                acts[r, pl.ds(pl.multiple_of(c * 128, 128), 128), :],
            ],
            axis=0,
        )

        @pl.loop(h * HS, (h + 1) * HS)
        def _(n):
            part = jnp.dot(
                rows, w[:, pl.ds(pl.multiple_of(n * NT, NT), NT)], preferred_element_type=F32
            )
            part = part - jnp.dot(
                hit[r], tbuf[:, pl.ds(pl.multiple_of(n * NT, NT), NT)], preferred_element_type=F32
            )
            sibs[r, n] = part[:128].astype(BF16)
            opart[r, n] = part[128:]
            remote(sibs.at[r, n], sibr.at[r, n], cs_s.at[r], cs_r.at[r, h], sib).start()

    def cols(n):
        return slice(n * NT, (n + 1) * NT)

    def steps(h):
        return range(h * HS, (h + 1) * HS)

    def chip_sum(r, q, n):
        rows = pl.ds(pl.multiple_of(q * PR, PR), PR)
        return opart[r, n, rows, :] + sibr[r, n, rows, :].astype(F32)

    def c_copy(r, h, src, dst, dev):
        return remote(
            ys.at[r, src, :, half(h)], yr.at[r, dst, :, half(h)], cy_s.at[r, h], cy_r.at[r, h], dev
        )

    def c_all(r, h):
        ref = ys.at[r, pl.ds(0, 7), :, half(h)]
        return remote(ref, ref, cy_s.at[r, h], cy_r.at[r, h], sib)

    def c_a(r, h):
        ref = sibr.at[r, pl.ds(h * HS, HS)]
        remote(ref, ref, cs_s.at[r], cs_r.at[r, h], sib).wait_recv()
        for q, dev in peers:
            for n in steps(h):
                ys[r, q, :, cols(n)] = chip_sum(r, q, n).astype(BF16)
            c_copy(r, h, q, place, dev).start()

    def place_targets():
        tbuf[2 * PR :, :] = jnp.zeros((128 - 2 * PR, D), BF16)
        own_rows = (
            lax.broadcasted_iota(jnp.int32, (ROWS, 128), 0)
            == lax.broadcasted_iota(jnp.int32, (ROWS, 128), 1) + 2 * PR * t
        ) & (lax.broadcasted_iota(jnp.int32, (ROWS, 128), 1) < 2 * PR)
        own_rows = own_rows.astype(F32).astype(BF16)
        row = lax.broadcasted_iota(jnp.int32, (CR, ROWS), 0)
        core = (row // 128 + 1 - c) % 2
        base = 2 * PR * (2 * ((row % 128) // PR) + core) + row % PR
        wanted = jnp.broadcast_to(order_ref[...], (CR, ROWS))
        for r in range(CH):
            found = (wanted == base + PR * r).astype(F32).astype(BF16)
            hit[r] = jnp.dot(found, own_rows, preferred_element_type=F32).astype(BF16)

    def c_d(r, h):
        c_all(r, h).wait_recv()
        for n in steps(h):
            total = chip_sum(r, place, n)
            for q, _ in peers:
                total = total + yr[r, q, :, cols(n)].astype(F32)
            resid = (total + db_ref[:, cols(n)]) * SCALE
            rbuf[r, own_core, :, cols(n)] = resid.astype(BF16)
        ar[r][h].start()

    def f_copy(r, k, src, slot, dev):
        return remote(src, frecv.at[r, slot], f_s.at[r, k], f_r.at[r, slot], dev)

    def f_wait(r, slot):
        remote(frecv.at[r, slot], frecv.at[r, slot], f_s.at[r, 0], f_r.at[r, slot], sib).wait_recv()

    def f_sends(r, name):
        def to_owner(l, base):
            return f_copy(r, l, gb.at[r, l], base + zl, (l, t))

        return {
            "a1": lambda: [to_owner(0, 0)],
            "s1": lambda: [to_owner(1, 0)],
            "a2": lambda: [
                f_copy(r, 0, gb.at[r, 0], 2, xup),
                f_copy(r, 1, gb.at[r, 1], 4, xdn),
            ],
            "a3": lambda: [f_copy(r, 3, gb.at[r, 3], 4, xup), f_copy(r, 2, gb.at[r, 2], 4, xdn)],
            "b2": lambda: [to_owner(3, 0)],
            "s2": lambda: [to_owner(2, 0)],
            "b3": lambda: [to_owner(4, 0), to_owner(5, 0)],
            "c3": lambda: [to_owner(1, 2)],
            "s3": lambda: [to_owner(0, 2)],
            "r0": lambda: [f_copy(r, 7, frecv.at[r, 4], 2 + zl, (3, t))],
        }[name]()

    def f_go(r, name, before=None):
        @pl.when(x == int(name[1]))
        def _():
            if before is not None:
                before()
            for cp in f_sends(r, name):
                cp.start()

    def grads(r, i):
        @pl.when(i <= x)
        def _():
            p = (i + x // 3) % 3 if i < 3 else 3
            g = lax.dot_general(
                rbuf[r].reshape(CR, D), w[pl.ds(pl.multiple_of(p * 2 * FS, 2 * FS), 2 * FS), :],
                NT_DIMS, preferred_element_type=F32,
            )

            @pl.when(x != i)
            def _():
                gb[r, 2 * p] = g[:, :FS].astype(BF16)
                gb[r, 2 * p + 1] = g[:, FS:].astype(BF16)

            @pl.when(x == i)
            def _():
                gown[r, 0] = g[:, :FS]
                gown[r, 1] = g[:, FS:] * zl.astype(F32)

        def add(pairs):
            def fn():
                for l, slot in pairs:
                    f_wait(r, slot)
                    gb[r, l] = (gb[r, l].astype(F32) + frecv[r, slot].astype(F32)).astype(BF16)

            return fn

        if i == 0:
            for name in ("a1", "a2", "a3"):
                f_go(r, name)
        if i == 1:
            f_go(r, "b2")
            f_go(r, "b3")
        if i == 2:
            f_go(r, "c3")

    def f_add(r):
        def add(l, slot):
            def fn():
                f_wait(r, slot)
                gb[r, l] = (gb[r, l].astype(F32) + frecv[r, slot].astype(F32)).astype(BF16)

            return fn

        f_go(r, "s1", add(1, 4))
        f_go(r, "s2", add(2, 4))
        f_go(r, "s3", add(0, 2))

    def f_relay(r):
        f_go(r, "r0", lambda: f_wait(r, 4))

    def f_zcopy(r):
        return remote(fzs.at[r], fzr.at[r], fz_s.at[r], fz_r.at[r], zpl)

    def f_own(r):
        @pl.when(zl == 1)
        def _():
            fzs[r] = gown[r, 0].astype(BF16)
            f_zcopy(r).start()

    def f_fin(r):
        gown[r, 0] = jnp.where(zl == 1, gown[r, 1], gown[r, 0])

        @pl.when(zl == 0)
        def _():
            f_zcopy(r).wait_recv()
            gown[r, 0] = gown[r, 0] + fzr[r].astype(F32)

        for cond, slots in ((x < 3, (0, 1)), ((x == 0) | (m == 3), (2, 3))):

            @pl.when(cond)
            def _(slots=slots):
                for slot in slots:
                    f_wait(r, slot)
                    gown[r, 0] = gown[r, 0] + frecv[r, slot].astype(F32)

        norm = no_ref[pl.ds(m, 1), :]
        grad = jnp.where(pre[r] > 0, gown[r, 0] + norm * SCALE, 0.0)
        go[r] = grad.astype(BF16)
        fsum = jnp.sum(grad, axis=0, keepdims=True)
        fo[...] = fsum if r == 0 else fo[...] + fsum

    def flip(r):
        @pl.loop(0, LAYERS)
        def _(l):
            block = acts[r, :, pl.ds(pl.multiple_of(l * FS, FS), FS)]
            act_t[l, :, r * CR : (r + 1) * CR] = block.T

    def dec_zero():
        for l in range(1, LAYERS):

            @pl.when(l > m)
            def _(l=l):
                do[l] = jnp.zeros((FS, D), BF16)

    def dec_grads(lo, hi):
        @pl.loop(lo, hi)
        def _(l):
            @pl.when(l <= m)
            def _():
                a_t = act_t[l]
                sums = jnp.dot(a_t, jnp.ones((ROWS, 128), BF16), preferred_element_type=F32)
                pick = (lax.broadcasted_iota(jnp.int32, (LAYERS, 128), 0) == l).astype(F32)
                norm = lax.dot_general(
                    no_ref[...], pick, TN_DIMS,
                    preferred_element_type=F32, precision=lax.Precision.HIGHEST,
                )
                factor = jnp.concatenate([sums * SCALE / norm] * 4, axis=1)
                rows = pl.ds(pl.multiple_of(l * FS, FS), FS)
                for n in range(NSTEPS):
                    part = jnp.dot(
                        a_t, rbuf[:, :, :, cols(n)].reshape(ROWS, NT), preferred_element_type=F32
                    )
                    do[l, :, cols(n)] = (part + factor * w[rows, cols(n)].astype(F32)).astype(BF16)

    def out_sum():
        ones = jnp.ones((8, ROWS), BF16)
        oo[...] = jnp.dot(ones, rbuf[...].reshape(ROWS, D), preferred_element_type=F32)[0:1]

    for k in range(2):
        local[k].wait()
    ax[0].start()
    clear()
    dec_zero()
    norms(0, 4)
    place_targets()
    ax[0].sent()
    ax[1].start()
    local[2].wait()
    local[3].wait()
    ax[0].take()
    ax[0].finish()
    encode(0)
    b_start(0)
    ax[1].take()
    b_step1(0)
    b_pass(0, b_relay_a)
    ax[1].finish()
    encode(1)
    b_start(1)
    norms(4, 8)
    b_pass(0, b_relay_b)
    b_step1(1)
    b_pass(1, b_relay_a)
    b_finish(0)
    decode(0, 0)
    c_a(0, 0)
    decode(0, 1)
    c_a(0, 1)
    b_pass(1, b_relay_b)
    c_d(0, 0)
    b_finish(1)
    c_d(0, 1)
    decode(1, 0)
    c_a(1, 0)
    decode(1, 1)
    c_a(1, 1)
    ar[0][0].take()
    ar[0][1].take()
    c_d(1, 0)
    ar[0][0].finish()
    ar[0][1].finish()
    grads(0, 0)
    c_d(1, 1)
    grads(0, 1)
    grads(0, 2)
    grads(0, 3)
    f_own(0)
    ar[1][0].take()
    ar[1][1].take()
    f_add(0)
    flip(0)
    norms_finish()
    ar[1][0].finish()
    ar[1][1].finish()
    grads(1, 0)
    grads(1, 1)
    grads(1, 2)
    f_relay(0)
    grads(1, 3)
    f_own(1)
    flip(1)
    out_sum()
    dec_grads(0, 1)
    f_add(1)
    dec_grads(1, 2)
    f_relay(1)
    f_fin(0)
    dec_grads(2, 8)
    f_fin(1)

    for g in ax + ar[0] + ar[1]:
        if g is not ax[0]:
            g.sent()
        g.drain()
    for r in range(CH):
        b_drain(r)
        remote(sibs.at[r], sibr.at[r], cs_s.at[r], cs_r.at[r, 0], sib).wait_send()
        for h in range(HALVES):
            c_all(r, h).wait_send()
        for name in ("a1", "s1", "a2", "a3", "b2", "s2", "b3", "c3", "s3", "r0"):

            @pl.when(x == int(name[1]))
            def _(name=name):
                for cp in f_sends(r, name):
                    cp.wait_send()

        pl.when(zl == 1)(f_zcopy(r).wait_send)
    norm_all().wait_send()


def run_main(x, tgt, order, we, eb, w, db):
    any_spec = pl.BlockSpec(memory_space=pl.ANY)
    vmem = pl.BlockSpec(memory_space=pltpu.VMEM)
    dma = pltpu.SemaphoreType.DMA
    return pl.pallas_call(
        main_kernel,
        out_shape=(
            pltpu.VMEM((CH, TOKS, PR, D), BF16),
            pltpu.VMEM((CH, CR, FS), BF16),
            pltpu.VMEM((LAYERS, FS, D), BF16),
            pltpu.VMEM((1, FS), F32),
            pltpu.VMEM((1, D), F32),
        ),
        in_specs=[any_spec, any_spec, vmem, any_spec, vmem, any_spec, vmem],
        out_specs=(vmem,) * 5,
        scratch_shapes=[
            pltpu.VMEM((128, D), BF16),
            pltpu.VMEM((CH, TOKS, PR, D), BF16),
            pltpu.VMEM((CH, CR, D), BF16),
            pltpu.VMEM((CH, CR, FS), BF16),
            pltpu.VMEM((CH, CR, FS), BF16),
            pltpu.VMEM((CH, CR, FS), F32),
            pltpu.VMEM((D, FS), BF16),
            pltpu.VMEM((LAYERS * FS, D), BF16),
            pltpu.VMEM((CH, NSTEPS, 128, NT), F32),
            pltpu.VMEM((CH, NSTEPS, 128, NT), BF16),
            pltpu.VMEM((CH, NSTEPS, 128, NT), BF16),
            pltpu.VMEM((CH, 8, PR, D), BF16),
            pltpu.VMEM((CH, 8, PR, D), BF16),
            pltpu.VMEM((CH, CR, 128), BF16),
            pltpu.VMEM((CH, LAYERS, CR, FS), BF16),
            pltpu.VMEM((CH, 2, CR, FS), F32),
            pltpu.VMEM((CH, 5, CR, FS), BF16),
            pltpu.VMEM((CH, CR, FS), BF16),
            pltpu.VMEM((CH, CR, FS), BF16),
            pltpu.VMEM((LAYERS, LAYERS, FS), F32),
            pltpu.VMEM((LAYERS, FS), F32),
            pltpu.VMEM((LAYERS, FS, ROWS), BF16),
            dma((4 + LAYERS,)), dma((CH + CH * HALVES, 2)), dma((CH + CH * HALVES, 2)),
            dma((CH, 9)), dma((CH, 10)), dma((CH,)), dma((CH, HALVES)),
            dma((CH, HALVES)), dma((CH, HALVES)),
            dma((CH, 8)), dma((CH, 5)), dma((CH,)), dma((CH,)),
            dma((1,)), dma((1,)),
        ],
        compiler_params=pltpu.CompilerParams(
            collective_id=0, has_side_effects=True, vmem_limit_bytes=46 << 20
        ),
        name="window",
    )(x, tgt, order, we, eb, w, db)


def tail_kernel(x_ref, g_ref, d_ref, f_ref, o_ref, dw_hbm, dwe_hbm, fg_hbm, og_hbm, enc, sems):
    copies = [
        pltpu.make_async_copy(d_ref.at[l], dw_hbm.at[0, l], sems.at[l]) for l in range(LAYERS)
    ]
    copies += [
        pltpu.make_async_copy(f_ref, fg_hbm, sems.at[LAYERS]),
        pltpu.make_async_copy(o_ref, og_hbm, sems.at[LAYERS + 1]),
    ]
    for cp in copies:
        cp.start()
    g = g_ref[...].reshape(ROWS, FS).T
    for n in range(NSTEPS):
        cs = slice(n * NT, (n + 1) * NT)
        part = jnp.dot(g, x_ref[:, :, :, cs].reshape(ROWS, NT), preferred_element_type=F32)
        enc[cs, :] = part.astype(BF16).T
    copies.append(pltpu.make_async_copy(enc, dwe_hbm.at[0], sems.at[LAYERS + 2]))
    copies[-1].start()
    for cp in copies:
        cp.wait()


def run_tail(xs, gl, dec, fg, og):
    any_spec = pl.BlockSpec(memory_space=pl.ANY)
    vmem = pl.BlockSpec(memory_space=pltpu.VMEM)
    return pl.pallas_call(
        tail_kernel,
        out_shape=(
            jax.ShapeDtypeStruct((1, LAYERS, FS, D), BF16),
            jax.ShapeDtypeStruct((1, D, FS), BF16),
            jax.ShapeDtypeStruct((1, FS), F32),
            jax.ShapeDtypeStruct((1, D), F32),
        ),
        in_specs=[vmem] * 5,
        out_specs=(any_spec,) * 4,
        scratch_shapes=[pltpu.VMEM((D, FS), BF16), pltpu.SemaphoreType.DMA((LAYERS + 3,))],
        compiler_params=pltpu.CompilerParams(vmem_limit_bytes=20 << 20),
        name="weights",
    )(xs, gl, dec, fg, og)


def on_device(x, tgt, order, we, eb, w, db):
    xs, gl, dec, fg, og = run_main(x, tgt, order[None], we, eb, w, db)
    dw, dwe, fg, og = run_tail(xs, gl, dec, fg, og)
    return dwe, fg, dw, og


def solution(mesh):
    placed = (
        P("layer", "tok", None),
        P("layer", "tok", None),
        P(),
        P("layer", None, "tok"),
        P("layer", "tok"),
        P("layer", None, "tok", None),
        P("layer", None),
    )
    return jax.shard_map(
        on_device,
        mesh=mesh,
        in_specs=placed,
        out_specs=(
            P("layer", None, "tok"),
            P("layer", "tok"),
            P("layer", None, "tok", None),
            P("layer", None),
        ),
        check_vma=False,
    )
```
